128 devices in a mesh: zone: 8 (over x, core), row: 16 (over y, z).
Axes of the slice: x: 4, y: 4, z: 4, core: 2. Of those that a mesh axis runs over, the one named last changes fastest.
Arguments:
- block_input: bfloat16 [512, 256, 1024], P('row', 'zone'), may hold values from -6 to 6
- cotangent: bfloat16 [512, 256, 1024], P('row', 'zone'), may hold values from -6 to 6
- w_up: bfloat16 [1024, 2048], replicated, may hold values from -0.1875 to 0.1875
- w_down: bfloat16 [2048, 1024], replicated, may hold values from -0.125 to 0.125
- ln_gain: float32 [1024], replicated, may hold values from 0.5 to 1.5
- pair_live: int32 [16, 8, 3], P('row', 'zone'), may hold values 0 or 1
- row_interp: bfloat16 [16, 8, 3, 32, 48], P('row', 'zone'), may hold values from -1 to 1
- col_interp: bfloat16 [16, 8, 3, 32, 48], P('row', 'zone'), may hold values from -1 to 1
Outputs:
- source_grad: bfloat16 [768, 384, 1024], P('row', 'zone')
- up_grad: float32 [1024, 2048], P(('zone', 'row'))
- down_grad: float32 [2048, 1024], P(('zone', 'row'))
- gain_grad: float32 [1024], P(('zone', 'row'))
The draws below stay inside these ranges and needn't reach their ends.
All inputs are finite; a program needn't handle non-finite values. No bound on the sum of `pair_live` on one device may be relied on, other than what follows from the above.
Results may differ from the reference program's by a relative error of at most 0.02.
Values may be sent and summed in bfloat16 or wider, within the bound.
A program may use at most 128 MiB of HBM per device.

```python
import math
import jax
import jax.numpy as jnp
from jax import lax

D = 1024
FF = 2048
TGT = 32
SRC = 48
NTR = 512
NTC = 256
NSR = 768
NSC = 384
TOKENS = 131072
N_ZONE = 8
N_ROW = 16


def with_ends(drawn, key, low, high):
    longest = drawn.shape.index(max(drawn.shape))
    spots = []
    for shift in (0, 1):
        where = [jax.random.randint(jax.random.fold_in(key, axis), (), 0, length) for axis, length in enumerate(drawn.shape)]
        where[longest] = (where[longest] + shift) % drawn.shape[longest]
        spots.append(tuple(where))
    return drawn.at[spots[0]].set(low).at[spots[1]].set(high)


def steps_of(stream_key, dims, shards, low, top_value):
    gain = 1.0
    for position, parts in shards:
        draws = jax.random.uniform(jax.random.fold_in(jax.random.fold_in(stream_key, 6), position), (parts,), jnp.float32, low / len(shards), top_value / len(shards))
        gain = gain * jnp.repeat(jnp.exp(draws), dims[position] // parts).reshape((-1,) + (1,) * (len(dims) - 1 - position))
    return gain


def centred(key, shape, width, bound, split=(), kind=jnp.bfloat16):
    drawn = width * jax.random.normal(key, shape, jnp.float32)
    if split:
        drawn = drawn * steps_of(key, shape, split, -0.22, 0.18)
    return jnp.clip(drawn, -bound, bound).astype(kind)


def setup_inputs(seed: int = 0) -> dict:
    key_of = jax.random.split(jax.random.key(seed), 9)
    block_input = centred(key_of[0], (NTR, NTC, D), 1.0, 6.0, ((0, 16), (1, 8)))
    cotangent = centred(key_of[1], (NTR, NTC, D), 1.0, 6.0, ((0, 16), (1, 8)))
    w_up = centred(key_of[2], (D, FF), D ** -0.5, 0.1875)
    w_down = centred(key_of[3], (FF, D), FF ** -0.5, 0.125)
    ln_gain = jnp.clip(1.0 + 0.1 * jax.random.normal(key_of[4], (D,), jnp.float32), 0.5, 1.5)
    pair_live = with_ends((jax.random.randint(key_of[5], (N_ROW, N_ZONE, 3), 0, 3) < 2).astype(jnp.int32), jax.random.fold_in(key_of[5], 1), 0, 1)
    row_interp = centred(key_of[6], (N_ROW, N_ZONE, 3, TGT, SRC), TGT ** -0.5, 1.0, ((0, 16), (1, 8)))
    col_interp = centred(key_of[7], (N_ROW, N_ZONE, 3, TGT, SRC), TGT ** -0.5, 1.0, ((0, 16), (1, 8)))
    return {"block_input": block_input, "cotangent": cotangent, "w_up": w_up, "w_down": w_down, "ln_gain": ln_gain, "pair_live": pair_live, "row_interp": row_interp, "col_interp": col_interp}


ROOT_HALF = 0.7071067811865476
INV_ROOT_TAU = 0.3989422804014327
epsilon = 1e-05

def gelu_value(pre):
    return pre * 0.5 * (1.0 + lax.erf(pre * ROOT_HALF))

def gelu_slope(pre):
    return 0.5 * (1.0 + lax.erf(pre * ROOT_HALF)) + pre * jnp.exp(-0.5 * pre * pre) * INV_ROOT_TAU

def mlp_backward(inputs, upstream, w_up, w_down, ln_gain):
    values = inputs.astype(jnp.float32)
    center = lax.optimization_barrier(jnp.mean(values, -1, keepdims=True))
    shifted = values - center
    spread = lax.optimization_barrier(jnp.mean(shifted * shifted, -1, keepdims=True))
    inv_std = lax.rsqrt(spread + epsilon)
    normal = shifted * inv_std
    normed = (normal * ln_gain).astype(jnp.bfloat16)
    pre = jnp.dot(normed, w_up, preferred_element_type=jnp.float32)
    activated = gelu_value(pre).astype(jnp.bfloat16)
    back_act = jnp.dot(upstream, w_down.T, preferred_element_type=jnp.float32)
    back_pre = (back_act * gelu_slope(pre)).astype(jnp.bfloat16)
    down_term = jnp.dot(activated.T, upstream, preferred_element_type=jnp.float32)
    up_term = jnp.dot(normed.T, back_pre, preferred_element_type=jnp.float32)
    back_norm = jnp.dot(back_pre, w_up.T, preferred_element_type=jnp.float32)
    gain_term = lax.optimization_barrier(jnp.sum(back_norm * normal, 0))
    scaled = back_norm * ln_gain
    grad_in = upstream.astype(jnp.float32) + inv_std * (scaled - lax.optimization_barrier(jnp.mean(scaled, -1, keepdims=True)) - normal * lax.optimization_barrier(jnp.mean(scaled * normal, -1, keepdims=True)))
    return (grad_in.astype(jnp.bfloat16), up_term, down_term, gain_term)

def reference(block_input, cotangent, w_up, w_down, ln_gain, pair_live, row_interp, col_interp):
    band_in = block_input.reshape(N_ROW, TGT * NTC, D)
    band_up = cotangent.reshape(N_ROW, TGT * NTC, D)

    def one_band(carry, items):
        grad_band, up_term, down_term, gain_term = mlp_backward(items[0], items[1], w_up, w_down, ln_gain)
        return ((carry[0] + up_term, carry[1] + down_term, carry[2] + gain_term), grad_band)
    start = (jnp.zeros((D, FF), jnp.float32), jnp.zeros((FF, D), jnp.float32), jnp.zeros((D,), jnp.float32))
    sums, grad_bands = lax.scan(one_band, start, (band_in, band_up))
    factor = 1.0 / math.sqrt(TOKENS)
    grid_grad = grad_bands.reshape(NTR, NTC, D)

    def source_band(source_row):
        total = jnp.zeros((N_ZONE, SRC, SRC, D), jnp.float32)
        for slot in range(3):
            target_row = source_row + 1 - slot
            valid = jnp.logical_and(target_row >= 0, target_row < N_ROW).astype(jnp.float32)
            clipped = jnp.clip(target_row, 0, N_ROW - 1).astype(jnp.int32)
            block = lax.dynamic_slice_in_dim(grid_grad, clipped * TGT, TGT, 0).reshape(TGT, N_ZONE, TGT, D)
            rows = lax.dynamic_index_in_dim(row_interp, clipped, 0, keepdims=False)[:, slot]
            cols = lax.dynamic_index_in_dim(col_interp, clipped, 0, keepdims=False)[:, slot]
            live = lax.dynamic_index_in_dim(pair_live, clipped, 0, keepdims=False)[:, slot]
            rows_live = rows * live.astype(jnp.bfloat16)[:, None, None]
            half = jnp.einsum('izjc,zjl->zilc', block.astype(jnp.float32), cols.astype(jnp.float32)).astype(jnp.bfloat16)
            piece = jnp.einsum('zim,zilc->zmlc', rows_live.astype(jnp.float32), half.astype(jnp.float32)).astype(jnp.bfloat16)
            total = total + piece.astype(jnp.float32) * valid
        return total.astype(jnp.bfloat16).transpose(1, 0, 2, 3).reshape(SRC, NSC, D)
    bands = lax.map(source_band, jnp.arange(N_ROW, dtype=jnp.int32))
    source_grad = bands.reshape(NSR, NSC, D)
    return (source_grad, sums[0] * factor, sums[1] * factor, sums[2] * factor)
```

```python
import functools
import math

import jax
import jax.numpy as jnp
from jax import lax
from jax.experimental import pallas as pl
from jax.experimental.pallas import tpu as pltpu
from jax.sharding import PartitionSpec as P

MESH = pl.DeviceIdType.MESH
BF = jnp.bfloat16
F32 = jnp.float32
ROOT_HALF = 0.7071067811865476
INV_ROOT_TAU = 0.3989422804014327
EPS = 1e-05
D = 1024
FF = 2048
TOK = 1024
CH = 256
NCH = TOK // CH
FB = 512
N_SEM = 64


def nt(a, b):
    return lax.dot_general(a, b, (((1,), (1,)), ((), ())), preferred_element_type=F32)


def tn(a, b):
    return lax.dot_general(a, b, (((0,), (0,)), ((), ())), preferred_element_type=F32)


def nn(a, b):
    return lax.dot_general(a, b, (((1,), (0,)), ((), ())), preferred_element_type=F32)


def front(
    factor,
    live_ref,
    x_hbm,
    ct_hbm,
    wu_hbm,
    wd_hbm,
    gain_ref,
    rowi_ref,
    coli_ref,
    gg_out,
    ga_out,
    gb_out,
    mats_out,
    up_out,
    down_out,
    gain_out,
    xv,
    ct,
    wu,
    wd,
    normed,
    act,
    bp,
    gg,
    normal,
    inv_s,
    bn_s,
    grad,
    part,
    xa,
    xb,
    tt,
    ya,
    yb,
    uu,
    za,
    zb,
    mats,
    mrecv,
    gacc,
    gsrc,
    grecv,
    in_sem,
    out_sem,
    send_sem,
    recv_sem,
    halo_send,
    halo_recv,
):
    zone = lax.axis_index("zone")
    row = lax.axis_index("row")
    x = zone // 2
    c = zone - 2 * x
    y = row // 4
    z = row - 4 * y

    def mod4(v):
        return lax.rem(v, 4)

    def dx(j):
        return (2 * mod4(x + j) + c, row)

    def dy(j):
        return (zone, 4 * mod4(y + j) + z)

    def dz(j):
        return (zone, 4 * y + mod4(z + j))

    pair = (2 * x + (1 - c), row)
    upper = (zone, lax.rem(row + 1, 16))
    lower = (zone, lax.rem(row + 15, 16))

    loads = []
    for n, (src, dst) in enumerate(
        [(x_hbm.at[pl.ds(0, CH)], xv.at[pl.ds(0, CH)]), (wu_hbm, wu),
         (ct_hbm.at[pl.ds(0, CH)], ct.at[pl.ds(0, CH)]), (wd_hbm, wd),
         (x_hbm.at[pl.ds(CH, TOK - CH)], xv.at[pl.ds(CH, TOK - CH)]),
         (ct_hbm.at[pl.ds(CH, TOK - CH)], ct.at[pl.ds(CH, TOK - CH)])]
    ):
        cp = pltpu.make_async_copy(src, dst, in_sem.at[n])
        cp.start()
        loads.append(cp)

    barrier = pltpu.get_barrier_semaphore()
    peers = [pair, upper, lower] + [f(j) for f in (dx, dy, dz) for j in (1, 2, 3)]
    for peer in peers:
        pl.semaphore_signal(barrier, inc=1, device_id=peer, device_id_type=MESH)

    counter = [0]

    def remote(src, dst, device):
        k = counter[0]
        counter[0] += 1
        return pltpu.make_async_remote_copy(
            src_ref=src, dst_ref=dst, send_sem=send_sem.at[k], recv_sem=recv_sem.at[k],
            device_id=device, device_id_type=MESH,
        )

    mats[...] = jnp.zeros_like(mats)
    for k in range(3):
        keep = live_ref[0, k]
        if k == 0:
            keep = jnp.where(row > 0, keep, 0)
        if k == 2:
            keep = jnp.where(row < 15, keep, 0)
        mats[k, 0, :, 0:48] = (rowi_ref[k].astype(F32) * keep.astype(F32)).astype(BF)
        mats[k, 1, :, 0:48] = coli_ref[k]
    gacc[...] = jnp.zeros_like(gacc)

    def chunk(t):
        rows = pl.ds(pl.multiple_of(t * CH, CH), CH)
        gain = gain_ref[...]

        @pl.loop(0, CH // 32)
        def _(s):
            r0 = pl.multiple_of(s * 32, 32)
            v = xv[pl.ds(pl.multiple_of(t * CH + r0, 32), 32), :].astype(F32)
            center = jnp.mean(v, -1, keepdims=True)
            sh = v - center
            inv = lax.rsqrt(jnp.mean(sh * sh, -1, keepdims=True) + EPS)
            nv = sh * inv
            normal[pl.ds(r0, 32), :] = nv
            inv_s[pl.ds(r0, 32), :] = jnp.broadcast_to(inv, (32, 128))
            normed[pl.ds(pl.multiple_of(t * CH + r0, 32), 32), :] = (nv * gain).astype(BF)

        @pl.loop(0, FF // FB)
        def _(f):
            cols = pl.ds(pl.multiple_of(f * FB, FB), FB)
            pre = nn(normed[rows, :], wu[:, cols])
            ba = nt(ct[rows, :], wd[cols, :])
            h = 0.5 * (1.0 + lax.erf(pre * ROOT_HALF))
            act[rows, cols] = (pre * h).astype(BF)
            bp[rows, cols] = (ba * (h + pre * jnp.exp(-0.5 * pre * pre) * INV_ROOT_TAU)).astype(BF)

        @pl.loop(0, D // FB)
        def _(f):
            cols = pl.ds(pl.multiple_of(f * FB, FB), FB)
            bn_s[:, cols] = nt(bp[rows, :], wu[cols, :])

        @pl.loop(0, CH // 32)
        def _(s):
            r0 = pl.multiple_of(s * 32, 32)
            r1 = pl.multiple_of(t * CH + r0, 32)
            bn = bn_s[pl.ds(r0, 32), :]
            nv = normal[pl.ds(r0, 32), :]
            inv = inv_s[pl.ds(r0, 32), 0:1]
            w = bn * nv
            gacc[...] += jnp.sum(w.reshape(4, 8, D), axis=0)
            scaled = bn * gain
            m1 = jnp.mean(scaled, -1, keepdims=True)
            m2 = jnp.mean(scaled * nv, -1, keepdims=True)
            g = ct[pl.ds(r1, 32), :].astype(F32) + inv * (scaled - m1 - nv * m2)
            gg[pl.ds(r1, 32), :] = g.astype(BF)

    def halo(t):
        rows = pl.ds(pl.multiple_of(t * CH, CH), CH)
        to_lower = pltpu.make_async_remote_copy(
            src_ref=gg.at[rows], dst_ref=ga_out.at[rows], send_sem=halo_send.at[0, t],
            recv_sem=halo_recv.at[0, t], device_id=lower, device_id_type=MESH)
        to_upper = pltpu.make_async_remote_copy(
            src_ref=gg.at[rows], dst_ref=gb_out.at[rows], send_sem=halo_send.at[1, t],
            recv_sem=halo_recv.at[1, t], device_id=upper, device_id_type=MESH)
        return to_lower, to_upper

    for cp in loads[:4]:
        cp.wait()
    chunk(0)
    pl.semaphore_wait(barrier, len(peers))
    m_low = remote(mats.at[0], mrecv.at[0], lower)
    m_upp = remote(mats.at[2], mrecv.at[1], upper)
    m_low.start()
    m_upp.start()
    for cp in halo(0):
        cp.start()
    for cp in loads[4:]:
        cp.wait()

    @pl.loop(1, NCH)
    def _(t):
        chunk(t)
        for cp in halo(t):
            cp.start()

    own = pltpu.make_async_copy(gg, gg_out, out_sem.at[0])
    own.start()

    gv = jnp.sum(gacc[...], axis=0, keepdims=True)
    gsrc[0] = jnp.concatenate([gv[:, 128 * i : 128 * (i + 1)] for i in range(8)], axis=0)
    g0 = remote(gsrc.at[0], grecv.at[0], pair)
    g0.start()

    order = [mod4(x + j) for j in (2, 1, 3, 0)]

    def up_tile(xq):
        feats = pl.ds(pl.multiple_of(xq * 256, 256), 256)

        @pl.loop(0, 4)
        def _(n):
            la = pl.ds(pl.multiple_of(n * 256, 256), 256)
            lb = pl.ds(pl.multiple_of(1024 + n * 256, 256), 256)
            left = tn(normed[:, feats], bp[:, la]).reshape(2, 16, 8, 256)
            right = tn(normed[:, feats], bp[:, lb]).reshape(2, 16, 8, 256)
            both = jnp.concatenate([left, right], axis=2).astype(BF)
            grad[0, pl.ds(2 * xq, 2), :, :, la] = both

    def down_tile(xq):
        hid = pl.ds(pl.multiple_of(xq * 512, 512), 512)

        @pl.loop(0, 4)
        def _(n):
            la = pl.ds(pl.multiple_of(n * 256, 256), 256)
            grad[1, pl.ds(2 * xq, 2), :, :, la] = (
                tn(act[:, hid], ct[:, la]).reshape(2, 16, 16, 256).astype(BF)
            )

    def add_into(dst, srcs, n):
        @pl.loop(0, n)
        def _(i):
            v = dst[i].astype(F32)
            for s in srcs:
                v = v + s[i].astype(F32)
            dst[i] = v.astype(BF)

    def add_to(out, srcs, n):
        @pl.loop(0, n)
        def _(i):
            v = srcs[0][i].astype(F32)
            for s in srcs[1:]:
                v = v + s[i].astype(F32)
            out[i] = v.astype(BF)

    xm, xp = mod4(x + 3), mod4(x + 1)
    ym, yp = mod4(y + 3), mod4(y + 1)
    zm, zp = mod4(z + 3), mod4(z + 1)
    p0 = [[None] * 4, [None] * 4]
    stage = [dict(), dict()]
    started = []

    def go(cp):
        cp.start()
        started.append(cp)
        return cp

    def tile(s, q):
        (up_tile if s == 0 else down_tile)(order[q])
        p0[s][q] = go(remote(grad.at[s, 2 * order[q] + (1 - c)], part.at[s, q], pair))

    def merge(s, q):
        p0[s][q].wait_recv()
        add_into(grad.at[s, 2 * order[q] + c], [part.at[s, q]], 16)

    def x_first(s):
        far = grad.at[s, 2 * order[0] + c]
        stage[s]["xa"] = [
            go(remote(far.at[pl.ds(0, 8)], xa.at[s, 0], dx(3))),
            go(remote(far.at[pl.ds(8, 8)], xa.at[s, 1], dx(1))),
        ]

    def x_second(s):
        low, high = grad.at[s, 2 * xm + c], grad.at[s, 2 * xp + c]
        stage[s]["xa"][0].wait_recv()
        add_into(low.at[pl.ds(0, 8)], [xa.at[s, 0]], 8)
        first = go(remote(low, xb.at[s, 0], dx(3)))
        stage[s]["xa"][1].wait_recv()
        add_into(high.at[pl.ds(8, 8)], [xa.at[s, 1]], 8)
        stage[s]["xb"] = [first, go(remote(high, xb.at[s, 1], dx(1)))]

    def x_done(s):
        for cp in stage[s]["xb"]:
            cp.wait_recv()
        add_to(tt.at[s], [grad.at[s, zone], xb.at[s, 0], xb.at[s, 1]], 16)

    def y_first(s):
        far = mod4(y + 2)
        stage[s]["ya"] = [
            go(remote(tt.at[s, pl.ds(4 * far, 2)], ya.at[s, 0], dy(3))),
            go(remote(tt.at[s, pl.ds(4 * far + 2, 2)], ya.at[s, 1], dy(1))),
        ]

    def y_second(s):
        stage[s]["ya"][0].wait_recv()
        add_into(tt.at[s, pl.ds(4 * ym, 2)], [ya.at[s, 0]], 2)
        first = go(remote(tt.at[s, pl.ds(4 * ym, 4)], yb.at[s, 0], dy(3)))
        stage[s]["ya"][1].wait_recv()
        add_into(tt.at[s, pl.ds(4 * yp + 2, 2)], [ya.at[s, 1]], 2)
        stage[s]["yb"] = [first, go(remote(tt.at[s, pl.ds(4 * yp, 4)], yb.at[s, 1], dy(1)))]

    def y_done(s):
        for cp in stage[s]["yb"]:
            cp.wait_recv()
        add_to(uu.at[s], [tt.at[s, pl.ds(4 * y, 4)], yb.at[s, 0], yb.at[s, 1]], 4)

    def z_first(s):
        far = uu.at[s, mod4(z + 2)]
        stage[s]["za"] = [
            go(remote(far.at[:, pl.ds(0, 512)], za.at[s, 0], dz(3))),
            go(remote(far.at[:, pl.ds(512, 512)], za.at[s, 1], dz(1))),
        ]

    def z_second(s):
        low, high = uu.at[s, zm], uu.at[s, zp]
        stage[s]["za"][0].wait_recv()
        low[:, 0:512] = (low[:, 0:512].astype(F32) + za[s, 0].astype(F32)).astype(BF)
        first = go(remote(low, zb.at[s, 0], dz(3)))
        stage[s]["za"][1].wait_recv()
        high[:, 512:1024] = (high[:, 512:1024].astype(F32) + za[s, 1].astype(F32)).astype(BF)
        stage[s]["zb"] = [first, go(remote(high, zb.at[s, 1], dz(1)))]

    def z_done(s):
        for cp in stage[s]["zb"]:
            cp.wait_recv()
        v = (uu[s, z].astype(F32) + zb[s, 0].astype(F32) + zb[s, 1].astype(F32)) * factor
        if s == 0:
            up_out[:, 0:1024] = v[0:8]
            up_out[:, 1024:2048] = v[8:16]
        else:
            down_out[...] = v

    gstage = {}

    def gain_send(axis_no, peer_of):
        gstage[axis_no] = [
            go(remote(gsrc.at[axis_no], grecv.at[3 * axis_no - 2 + j], peer_of(j + 1))) for j in range(3)
        ]

    def gain_sum(axis_no):
        v = gsrc[axis_no]
        for j, cp in enumerate(gstage[axis_no]):
            cp.wait_recv()
            v = v + grecv[3 * axis_no - 2 + j]
        gsrc[axis_no + 1] = v

    tile(0, 0)
    tile(0, 1)
    merge(0, 0)
    x_first(0)
    tile(0, 2)
    merge(0, 1)
    tile(0, 3)
    merge(0, 2)
    x_second(0)
    tile(1, 0)
    tile(1, 1)
    merge(1, 0)
    x_first(1)
    merge(0, 3)
    tile(1, 2)
    merge(1, 1)
    tile(1, 3)
    merge(1, 2)
    merge(1, 3)
    g0.wait_recv()
    gsrc[1] = gsrc[0] + grecv[0]
    gain_send(1, dx)
    x_second(1)
    gain_sum(1)
    gain_send(2, dy)
    x_done(0)
    y_first(0)
    gain_sum(2)
    gain_send(3, dz)
    y_second(0)
    y_done(0)
    z_first(0)
    gain_sum(3)
    z_second(0)
    x_done(1)
    y_first(1)
    z_done(0)
    y_second(1)
    y_done(1)
    z_first(1)
    z_second(1)
    z_done(1)

    sub = lax.broadcasted_iota(jnp.int32, (8, 128), 0)
    lane = lax.broadcasted_iota(jnp.int32, (8, 128), 1)
    line = jnp.sum(jnp.where(sub == zone, gsrc[4], 0.0), axis=0, keepdims=True)
    gain_out[...] = factor * jnp.sum(
        jnp.where(lane == 8 * row + sub, jnp.broadcast_to(line, (8, 128)), 0.0), axis=1, keepdims=True)

    m_low.wait()
    m_upp.wait()
    mats_out[0] = mrecv[0]
    mats_out[1] = mats[1]
    mats_out[2] = mrecv[1]
    for t in range(NCH):
        for cp in halo(t):
            cp.wait()
    own.wait()
    g0.wait_send()
    for cp in started:
        cp.wait_send()


def back(mats_ref, ga, gg, gb, out, b1, b2, half):
    @pl.when(pl.program_id(0) == 0)
    def _():
        r = lax.broadcasted_iota(jnp.int32, (384, 128), 0)
        q = lax.broadcasted_iota(jnp.int32, (384, 128), 1)
        pick_l = jnp.where(q == (r // 64) * 8 + r % 8, 1.0, 0.0).astype(BF)
        pick_m = jnp.where(q == r // 8, 1.0, 0.0).astype(BF)
        a = lax.broadcasted_iota(jnp.int32, (32, 256), 0)
        b = lax.broadcasted_iota(jnp.int32, (32, 256), 1)
        rep_j = jnp.where(b % 32 == a, 1.0, 0.0).astype(BF)
        rep_i = jnp.where(b // 8 == a, 1.0, 0.0).astype(BF)
        rr = lax.broadcasted_iota(jnp.int32, (384, 256), 0)
        cc = lax.broadcasted_iota(jnp.int32, (384, 256), 1)
        same_i = (rr // 8) % 8 == cc // 32
        same_l = rr % 8 == cc % 8
        for k in range(3):
            col = nt(pick_l, mats_ref[k, 1]).astype(BF)
            b1[k] = jnp.where(same_i, nn(col, rep_j), 0.0).astype(BF)
            rw = nt(pick_m, mats_ref[k, 0]).astype(BF)
            b2[:, k * 256 : (k + 1) * 256] = jnp.where(same_l, nn(rw, rep_i), 0.0).astype(BF)

    for k, src in enumerate((ga, gg, gb)):
        for g in range(4):
            h = nn(b1[k], src[g * 256 : (g + 1) * 256, :]).astype(BF)
            for lb in range(6):
                half[lb, k * 256 + g * 64 : k * 256 + (g + 1) * 64, :] = h[lb * 64 : (lb + 1) * 64]
    for lp in range(3):
        a = nn(b2[...], half[2 * lp]).reshape(48, 8, -1)
        b = nn(b2[...], half[2 * lp + 1]).reshape(48, 8, -1)
        out[:, lp * 16 : (lp + 1) * 16, :] = jnp.concatenate([a, b], axis=1).astype(BF)


def on_device(block_input, cotangent, w_up, w_down, ln_gain, pair_live, row_interp, col_interp):
    factor = 1.0 / math.sqrt(TOK * lax.axis_size("zone") * lax.axis_size("row"))
    hbm = pl.BlockSpec(memory_space=pl.ANY)
    vmem = pl.BlockSpec(memory_space=pltpu.VMEM)
    smem = pl.BlockSpec(memory_space=pltpu.SMEM)
    sds = jax.ShapeDtypeStruct
    grid_shape = sds((TOK, D), BF)
    gg, ga, gb, mats, up, down, gain = pl.pallas_call(
        functools.partial(front, factor),
        name="front",
        out_shape=(grid_shape, grid_shape, grid_shape, sds((3, 2, 32, 128), BF),
                   sds((8, FF), F32), sds((16, D), F32), sds((8, 1), F32)),
        in_specs=[smem, hbm, hbm, hbm, hbm, vmem, vmem, vmem],
        out_specs=(hbm, hbm, hbm, vmem, vmem, vmem, vmem),
        scratch_shapes=[
            pltpu.VMEM((TOK, D), BF),
            pltpu.VMEM((TOK, D), BF),
            pltpu.VMEM((D, FF), BF),
            pltpu.VMEM((FF, D), BF),
            pltpu.VMEM((TOK, D), BF),
            pltpu.VMEM((TOK, FF), BF),
            pltpu.VMEM((TOK, FF), BF),
            pltpu.VMEM((TOK, D), BF),
            pltpu.VMEM((CH, D), F32),
            pltpu.VMEM((CH, 128), F32),
            pltpu.VMEM((CH, D), F32),
            pltpu.VMEM((2, 8, 16, 16, 1024), BF),
            pltpu.VMEM((2, 4, 16, 16, 1024), BF),
            pltpu.VMEM((2, 2, 8, 16, 1024), BF),
            pltpu.VMEM((2, 2, 16, 16, 1024), BF),
            pltpu.VMEM((2, 16, 16, 1024), BF),
            pltpu.VMEM((2, 2, 2, 16, 1024), BF),
            pltpu.VMEM((2, 2, 4, 16, 1024), BF),
            pltpu.VMEM((2, 4, 16, 1024), BF),
            pltpu.VMEM((2, 2, 16, 512), BF),
            pltpu.VMEM((2, 2, 16, 1024), BF),
            pltpu.VMEM((3, 2, 32, 128), BF),
            pltpu.VMEM((2, 2, 32, 128), BF),
            pltpu.VMEM((8, D), F32),
            pltpu.VMEM((5, 8, 128), F32),
            pltpu.VMEM((10, 8, 128), F32),
            pltpu.SemaphoreType.DMA((6,)),
            pltpu.SemaphoreType.DMA((1,)),
            pltpu.SemaphoreType.DMA((N_SEM,)),
            pltpu.SemaphoreType.DMA((N_SEM,)),
            pltpu.SemaphoreType.DMA((2, NCH)),
            pltpu.SemaphoreType.DMA((2, NCH)),
        ],
        compiler_params=pltpu.CompilerParams(
            collective_id=0, has_side_effects=True, vmem_limit_bytes=60 * 1024 * 1024
        ),
    )(
        pair_live[0],
        block_input.reshape(TOK, D),
        cotangent.reshape(TOK, D),
        w_up,
        w_down,
        ln_gain.reshape(1, D),
        row_interp[0, 0],
        col_interp[0, 0],
    )
    lanes = 256
    source = pl.pallas_call(
        back,
        name="back",
        grid=(D // lanes,),
        out_shape=sds((48, 48, D), BF),
        in_specs=[pl.BlockSpec((3, 2, 32, 128), lambda i: (0, 0, 0, 0))]
        + [pl.BlockSpec((TOK, lanes), lambda i: (0, i))] * 3,
        out_specs=pl.BlockSpec((48, 48, lanes), lambda i: (0, 0, i)),
        scratch_shapes=[
            pltpu.VMEM((3, 384, 256), BF),
            pltpu.VMEM((384, 768), BF),
            pltpu.VMEM((6, 768, lanes), BF),
        ],
        compiler_params=pltpu.CompilerParams(dimension_semantics=("arbitrary",)),
    )(mats, ga, gg, gb)
    return source, up, down, gain.reshape(8)


def solution(mesh):
    in_specs = (
        P("row", "zone", None),
        P("row", "zone", None),
        P(),
        P(),
        P(),
        P("row", "zone", None),
        P("row", "zone", None, None, None),
        P("row", "zone", None, None, None),
    )
    out_specs = (
        P("row", "zone", None),
        P(("zone", "row"), None),
        P(("zone", "row"), None),
        P(("zone", "row")),
    )
    return jax.shard_map(
        on_device, mesh=mesh, in_specs=in_specs, out_specs=out_specs, check_vma=False
    )
```

```python
import functools
import math

import jax
import jax.numpy as jnp
from jax import lax
from jax.experimental import pallas as pl
from jax.experimental.pallas import tpu as pltpu
from jax.sharding import PartitionSpec as P

MESH = pl.DeviceIdType.MESH
BF = jnp.bfloat16
F32 = jnp.float32
ROOT_HALF = 0.7071067811865476
INV_ROOT_TAU = 0.3989422804014327
EPS = 1e-05
D = 1024
FF = 2048
TOK = 1024
CH = 256
NCH = TOK // CH
FB = 1024
NB = 1024
LN = 512
N_SEM = 64


def nt(a, b):
    return lax.dot_general(a, b, (((1,), (1,)), ((), ())), preferred_element_type=F32)


def tn(a, b):
    return lax.dot_general(a, b, (((0,), (0,)), ((), ())), preferred_element_type=F32)


def nn(a, b):
    return lax.dot_general(a, b, (((1,), (0,)), ((), ())), preferred_element_type=F32)


def front(
    factor,
    live_ref,
    x_hbm,
    ct_hbm,
    wu_hbm,
    wd_hbm,
    gain_ref,
    rowi_ref,
    coli_ref,
    gg_out,
    ga_out,
    gb_out,
    mats_out,
    up_out,
    down_out,
    gain_out,
    xv,
    ct,
    wu,
    wd,
    normed,
    normed_t,
    act_t,
    bp,
    gg,
    normal,
    inv_s,
    bn_s,
    grad,
    part,
    xa,
    xb,
    tt,
    ya,
    yb,
    uu,
    za,
    zb,
    mats,
    mrecv,
    gacc,
    gsrc,
    grecv,
    in_sem,
    out_sem,
    send_sem,
    recv_sem,
    halo_send,
    halo_recv,
):
    zone = lax.axis_index("zone")
    row = lax.axis_index("row")
    x = zone // 2
    c = zone - 2 * x
    y = row // 4
    z = row - 4 * y

    def mod4(v):
        return lax.rem(v, 4)

    def dx(j):
        return (2 * mod4(x + j) + c, row)

    def dy(j):
        return (zone, 4 * mod4(y + j) + z)

    def dz(j):
        return (zone, 4 * y + mod4(z + j))

    pair = (2 * x + (1 - c), row)
    upper = (zone, lax.rem(row + 1, 16))
    lower = (zone, lax.rem(row + 15, 16))

    loads = []
    for n, (src, dst) in enumerate(
        [(x_hbm.at[pl.ds(0, CH)], xv.at[pl.ds(0, CH)]), (wu_hbm, wu),
         (ct_hbm.at[pl.ds(0, CH)], ct.at[pl.ds(0, CH)]), (wd_hbm, wd),
         (x_hbm.at[pl.ds(CH, TOK - CH)], xv.at[pl.ds(CH, TOK - CH)]),
         (ct_hbm.at[pl.ds(CH, TOK - CH)], ct.at[pl.ds(CH, TOK - CH)])]
    ):
        cp = pltpu.make_async_copy(src, dst, in_sem.at[n])
        cp.start()
        loads.append(cp)

    barrier = pltpu.get_barrier_semaphore()
    peers = [pair, upper, lower] + [f(j) for f in (dx, dy, dz) for j in (1, 2, 3)]
    for peer in peers:
        pl.semaphore_signal(barrier, inc=1, device_id=peer, device_id_type=MESH)

    counter = [0]

    def remote(src, dst, device):
        k = counter[0]
        counter[0] += 1
        return pltpu.make_async_remote_copy(
            src_ref=src, dst_ref=dst, send_sem=send_sem.at[k], recv_sem=recv_sem.at[k],
            device_id=device, device_id_type=MESH,
        )

    mats[...] = jnp.zeros_like(mats)
    for k in range(3):
        keep = live_ref[0, k]
        if k == 0:
            keep = jnp.where(row > 0, keep, 0)
        if k == 2:
            keep = jnp.where(row < 15, keep, 0)
        mats[k, 0, :, 0:48] = (rowi_ref[k].astype(F32) * keep.astype(F32)).astype(BF)
        mats[k, 1, :, 0:48] = coli_ref[k]
    gacc[...] = jnp.zeros_like(gacc)

    def forward(start, m):
        gain = gain_ref[...]
        base = start % 512

        for s in range(m // CH):
            r0, r1 = base + s * CH, start + s * CH
            v = xv[r1 : r1 + CH, :].astype(F32)
            center = jnp.mean(v, -1, keepdims=True)
            sh = v - center
            inv = lax.rsqrt(jnp.mean(sh * sh, -1, keepdims=True) + EPS)
            nv = sh * inv
            normal[r0 : r0 + CH, :] = nv
            inv_s[r0 : r0 + CH, :] = jnp.broadcast_to(inv, (CH, 128))
            nb = (nv * gain).astype(BF)
            normed[r0 : r0 + CH, :] = nb
            normed_t[:, r1 : r1 + CH] = nb.T

        @pl.loop(0, FF // FB)
        def _(f):
            cols = pl.ds(pl.multiple_of(f * FB, FB), FB)
            pre = nn(normed[base : base + m, :], wu[:, cols])
            ba = nt(ct[start : start + m, :], wd[cols, :])
            h = 0.5 * (1.0 + lax.erf(pre * ROOT_HALF))
            act_t[cols, start : start + m] = (pre * h).astype(BF).T
            bp[start : start + m, cols] = (
                ba * (h + pre * jnp.exp(-0.5 * pre * pre) * INV_ROOT_TAU)
            ).astype(BF)

    def backward(start):
        gain = gain_ref[...]
        base = start % 512

        @pl.loop(0, D // NB)
        def _(f):
            cols = pl.ds(pl.multiple_of(f * NB, NB), NB)
            bn_s[:, cols] = nt(bp[start : start + CH, :], wu[cols, :])

        bn = bn_s[...]
        nv = normal[base : base + CH, :]
        inv = inv_s[base : base + CH, 0:1]
        gacc[...] += jnp.sum((bn * nv).reshape(CH // 8, 8, D), axis=0)
        scaled = bn * gain
        m1 = jnp.mean(scaled, -1, keepdims=True)
        m2 = jnp.mean(scaled * nv, -1, keepdims=True)
        g = ct[start : start + CH, :].astype(F32) + inv * (scaled - m1 - nv * m2)
        gg[start : start + CH, :] = g.astype(BF)

    def halo(t):
        rows = pl.ds(t * CH, CH)
        to_lower = pltpu.make_async_remote_copy(
            src_ref=gg.at[rows], dst_ref=ga_out.at[rows], send_sem=halo_send.at[0, t],
            recv_sem=halo_recv.at[0, t], device_id=lower, device_id_type=MESH)
        to_upper = pltpu.make_async_remote_copy(
            src_ref=gg.at[rows], dst_ref=gb_out.at[rows], send_sem=halo_send.at[1, t],
            recv_sem=halo_recv.at[1, t], device_id=upper, device_id_type=MESH)
        return to_lower, to_upper

    for cp in loads[:4]:
        cp.wait()
    forward(0, CH)
    backward(0)
    pl.semaphore_wait(barrier, len(peers))
    m_low = remote(mats.at[0], mrecv.at[0], lower)
    m_upp = remote(mats.at[2], mrecv.at[1], upper)
    m_low.start()
    m_upp.start()
    for cp in halo(0):
        cp.start()
    for cp in loads[4:]:
        cp.wait()
    forward(CH, CH)
    backward(CH)
    for cp in halo(1):
        cp.start()
    forward(2 * CH, 2 * CH)

    order = [mod4(x + j) for j in (2, 1, 3, 0)]

    def up_tiles(xa_, xb_):
        fa = pl.ds(pl.multiple_of(xa_ * 256, 256), 256)
        fb = pl.ds(pl.multiple_of(xb_ * 256, 256), 256)

        @pl.loop(0, 1024 // LN)
        def _(n):
            la = pl.ds(pl.multiple_of(n * LN, LN), LN)
            lb = pl.ds(pl.multiple_of(1024 + n * LN, LN), LN)
            lhs = jnp.concatenate([normed_t[fa, :], normed_t[fb, :]], axis=0)
            left = nn(lhs, bp[:, la]).reshape(4, 16, 8, LN)
            right = nn(lhs, bp[:, lb]).reshape(4, 16, 8, LN)
            both = jnp.concatenate([left, right], axis=2).astype(BF)
            grad[0, pl.ds(2 * xa_, 2), :, :, la] = both[0:2]
            grad[0, pl.ds(2 * xb_, 2), :, :, la] = both[2:4]

    def down_tile(xq):
        hid = pl.ds(pl.multiple_of(xq * 512, 512), 512)

        @pl.loop(0, 1024 // LN)
        def _(n):
            la = pl.ds(pl.multiple_of(n * LN, LN), LN)
            grad[1, pl.ds(2 * xq, 2), :, :, la] = (
                nn(act_t[hid, :], ct[:, la]).reshape(2, 16, 16, LN).astype(BF)
            )

    def add_into(dst, srcs, n):
        @pl.loop(0, n)
        def _(i):
            v = dst[i].astype(F32)
            for s in srcs:
                v = v + s[i].astype(F32)
            dst[i] = v.astype(BF)

    def add_to(out, srcs, n):
        @pl.loop(0, n)
        def _(i):
            v = srcs[0][i].astype(F32)
            for s in srcs[1:]:
                v = v + s[i].astype(F32)
            out[i] = v.astype(BF)

    xm, xp = mod4(x + 3), mod4(x + 1)
    ym, yp = mod4(y + 3), mod4(y + 1)
    zm, zp = mod4(z + 3), mod4(z + 1)
    p0 = [[None] * 4, [None] * 4]
    stage = [dict(), dict()]
    started = []

    def go(cp):
        cp.start()
        started.append(cp)
        return cp

    def send_pair(s, q):
        p0[s][q] = go(remote(grad.at[s, 2 * order[q] + (1 - c)], part.at[s, q], pair))

    def merge(s, q):
        p0[s][q].wait_recv()
        add_into(grad.at[s, 2 * order[q] + c], [part.at[s, q]], 16)

    def x_first(s):
        far = grad.at[s, 2 * order[0] + c]
        stage[s]["xa"] = [
            go(remote(far.at[pl.ds(0, 8)], xa.at[s, 0], dx(3))),
            go(remote(far.at[pl.ds(8, 8)], xa.at[s, 1], dx(1))),
        ]

    def x_second(s):
        low, high = grad.at[s, 2 * xm + c], grad.at[s, 2 * xp + c]
        stage[s]["xa"][0].wait_recv()
        add_into(low.at[pl.ds(0, 8)], [xa.at[s, 0]], 8)
        first = go(remote(low, xb.at[s, 0], dx(3)))
        stage[s]["xa"][1].wait_recv()
        add_into(high.at[pl.ds(8, 8)], [xa.at[s, 1]], 8)
        stage[s]["xb"] = [first, go(remote(high, xb.at[s, 1], dx(1)))]

    def x_done(s):
        for cp in stage[s]["xb"]:
            cp.wait_recv()
        add_to(tt.at[s], [grad.at[s, zone], xb.at[s, 0], xb.at[s, 1]], 16)

    def y_first(s):
        far = mod4(y + 2)
        stage[s]["ya"] = [
            go(remote(tt.at[s, pl.ds(4 * far, 2)], ya.at[s, 0], dy(3))),
            go(remote(tt.at[s, pl.ds(4 * far + 2, 2)], ya.at[s, 1], dy(1))),
        ]

    def y_second(s):
        stage[s]["ya"][0].wait_recv()
        add_into(tt.at[s, pl.ds(4 * ym, 2)], [ya.at[s, 0]], 2)
        first = go(remote(tt.at[s, pl.ds(4 * ym, 4)], yb.at[s, 0], dy(3)))
        stage[s]["ya"][1].wait_recv()
        add_into(tt.at[s, pl.ds(4 * yp + 2, 2)], [ya.at[s, 1]], 2)
        stage[s]["yb"] = [first, go(remote(tt.at[s, pl.ds(4 * yp, 4)], yb.at[s, 1], dy(1)))]

    def y_done(s):
        for cp in stage[s]["yb"]:
            cp.wait_recv()
        add_to(uu.at[s], [tt.at[s, pl.ds(4 * y, 4)], yb.at[s, 0], yb.at[s, 1]], 4)

    def z_first(s):
        far = uu.at[s, mod4(z + 2)]
        stage[s]["za"] = [
            go(remote(far.at[:, pl.ds(0, 512)], za.at[s, 0], dz(3))),
            go(remote(far.at[:, pl.ds(512, 512)], za.at[s, 1], dz(1))),
        ]

    def z_second(s):
        low, high = uu.at[s, zm], uu.at[s, zp]
        stage[s]["za"][0].wait_recv()
        low[:, 0:512] = (low[:, 0:512].astype(F32) + za[s, 0].astype(F32)).astype(BF)
        first = go(remote(low, zb.at[s, 0], dz(3)))
        stage[s]["za"][1].wait_recv()
        high[:, 512:1024] = (high[:, 512:1024].astype(F32) + za[s, 1].astype(F32)).astype(BF)
        stage[s]["zb"] = [first, go(remote(high, zb.at[s, 1], dz(1)))]

    def z_done(s):
        for cp in stage[s]["zb"]:
            cp.wait_recv()
        v = (uu[s, z].astype(F32) + zb[s, 0].astype(F32) + zb[s, 1].astype(F32)) * factor
        if s == 0:
            up_out[:, 0:1024] = v[0:8]
            up_out[:, 1024:2048] = v[8:16]
        else:
            down_out[...] = v

    gstage = {}

    def gain_send(axis_no, peer_of):
        gstage[axis_no] = [
            go(remote(gsrc.at[axis_no], grecv.at[3 * axis_no - 2 + j], peer_of(j + 1))) for j in range(3)
        ]

    def gain_sum(axis_no):
        v = gsrc[axis_no]
        for j, cp in enumerate(gstage[axis_no]):
            cp.wait_recv()
            v = v + grecv[3 * axis_no - 2 + j]
        gsrc[axis_no + 1] = v

    up_tiles(order[0], order[1])
    send_pair(0, 0)
    send_pair(0, 1)
    up_tiles(order[2], order[3])
    send_pair(0, 2)
    send_pair(0, 3)
    merge(0, 0)
    x_first(0)
    backward(2 * CH)
    for cp in halo(2):
        cp.start()
    merge(0, 1)
    merge(0, 2)
    x_second(0)
    down_tile(order[0])
    send_pair(1, 0)
    down_tile(order[1])
    send_pair(1, 1)
    merge(0, 3)
    merge(1, 0)
    x_first(1)
    down_tile(order[2])
    send_pair(1, 2)
    down_tile(order[3])
    send_pair(1, 3)
    merge(1, 1)
    backward(3 * CH)
    for cp in halo(3):
        cp.start()
    own = pltpu.make_async_copy(gg, gg_out, out_sem.at[0])
    own.start()
    gv = jnp.sum(gacc[...], axis=0, keepdims=True)
    gsrc[0] = jnp.concatenate([gv[:, 128 * i : 128 * (i + 1)] for i in range(8)], axis=0)
    g0 = remote(gsrc.at[0], grecv.at[0], pair)
    g0.start()
    merge(1, 2)
    merge(1, 3)
    x_second(1)
    g0.wait_recv()
    gsrc[1] = gsrc[0] + grecv[0]
    gain_send(1, dx)
    gain_sum(1)
    gain_send(2, dy)
    x_done(0)
    y_first(0)
    gain_sum(2)
    gain_send(3, dz)
    y_second(0)
    y_done(0)
    z_first(0)
    gain_sum(3)
    z_second(0)
    x_done(1)
    y_first(1)
    z_done(0)
    y_second(1)
    y_done(1)
    z_first(1)
    z_second(1)
    z_done(1)

    sub = lax.broadcasted_iota(jnp.int32, (8, 128), 0)
    lane = lax.broadcasted_iota(jnp.int32, (8, 128), 1)
    line = jnp.sum(jnp.where(sub == zone, gsrc[4], 0.0), axis=0, keepdims=True)
    gain_out[...] = factor * jnp.sum(
        jnp.where(lane == 8 * row + sub, jnp.broadcast_to(line, (8, 128)), 0.0), axis=1, keepdims=True)

    m_low.wait()
    m_upp.wait()
    mats_out[0] = mrecv[0]
    mats_out[1] = mats[1]
    mats_out[2] = mrecv[1]
    for t in range(NCH):
        for cp in halo(t):
            cp.wait()
    own.wait()
    g0.wait_send()
    for cp in started:
        cp.wait_send()


def back(mats_ref, ga, gg, gb, out, b1, b2, half):
    @pl.when(pl.program_id(0) == 0)
    def _():
        r = lax.broadcasted_iota(jnp.int32, (384, 128), 0)
        q = lax.broadcasted_iota(jnp.int32, (384, 128), 1)
        pick_l = jnp.where(q == (r // 64) * 8 + r % 8, 1.0, 0.0).astype(BF)
        pick_m = jnp.where(q == r // 8, 1.0, 0.0).astype(BF)
        a = lax.broadcasted_iota(jnp.int32, (32, 256), 0)
        b = lax.broadcasted_iota(jnp.int32, (32, 256), 1)
        rep_j = jnp.where(b % 32 == a, 1.0, 0.0).astype(BF)
        rep_i = jnp.where(b // 8 == a, 1.0, 0.0).astype(BF)
        rr = lax.broadcasted_iota(jnp.int32, (384, 256), 0)
        cc = lax.broadcasted_iota(jnp.int32, (384, 256), 1)
        same_i = (rr // 8) % 8 == cc // 32
        same_l = rr % 8 == cc % 8
        for k in range(3):
            col = nt(pick_l, mats_ref[k, 1]).astype(BF)
            b1[k] = jnp.where(same_i, nn(col, rep_j), 0.0).astype(BF)
            rw = nt(pick_m, mats_ref[k, 0]).astype(BF)
            b2[:, k * 256 : (k + 1) * 256] = jnp.where(same_l, nn(rw, rep_i), 0.0).astype(BF)

    for k, src in enumerate((ga, gg, gb)):
        for g in range(4):
            h = nn(b1[k], src[g * 256 : (g + 1) * 256, :]).astype(BF)
            for lb in range(6):
                half[lb, k * 256 + g * 64 : k * 256 + (g + 1) * 64, :] = h[lb * 64 : (lb + 1) * 64]
    for lp in range(3):
        a = nn(b2[...], half[2 * lp]).reshape(48, 8, -1)
        b = nn(b2[...], half[2 * lp + 1]).reshape(48, 8, -1)
        out[:, lp * 16 : (lp + 1) * 16, :] = jnp.concatenate([a, b], axis=1).astype(BF)


def on_device(block_input, cotangent, w_up, w_down, ln_gain, pair_live, row_interp, col_interp):
    factor = 1.0 / math.sqrt(TOK * lax.axis_size("zone") * lax.axis_size("row"))
    hbm = pl.BlockSpec(memory_space=pl.ANY)
    vmem = pl.BlockSpec(memory_space=pltpu.VMEM)
    smem = pl.BlockSpec(memory_space=pltpu.SMEM)
    sds = jax.ShapeDtypeStruct
    grid_shape = sds((TOK, D), BF)
    gg, ga, gb, mats, up, down, gain = pl.pallas_call(
        functools.partial(front, factor),
        name="front",
        out_shape=(grid_shape, grid_shape, grid_shape, sds((3, 2, 32, 128), BF),
                   sds((8, FF), F32), sds((16, D), F32), sds((8, 1), F32)),
        in_specs=[smem, hbm, hbm, hbm, hbm, vmem, vmem, vmem],
        out_specs=(hbm, hbm, hbm, vmem, vmem, vmem, vmem),
        scratch_shapes=[
            pltpu.VMEM((TOK, D), BF),
            pltpu.VMEM((TOK, D), BF),
            pltpu.VMEM((D, FF), BF),
            pltpu.VMEM((FF, D), BF),
            pltpu.VMEM((512, D), BF),
            pltpu.VMEM((D, TOK), BF),
            pltpu.VMEM((FF, TOK), BF),
            pltpu.VMEM((TOK, FF), BF),
            pltpu.VMEM((TOK, D), BF),
            pltpu.VMEM((512, D), F32),
            pltpu.VMEM((512, 128), F32),
            pltpu.VMEM((CH, D), F32),
            pltpu.VMEM((2, 8, 16, 16, 1024), BF),
            pltpu.VMEM((2, 4, 16, 16, 1024), BF),
            pltpu.VMEM((2, 2, 8, 16, 1024), BF),
            pltpu.VMEM((2, 2, 16, 16, 1024), BF),
            pltpu.VMEM((2, 16, 16, 1024), BF),
            pltpu.VMEM((2, 2, 2, 16, 1024), BF),
            pltpu.VMEM((2, 2, 4, 16, 1024), BF),
            pltpu.VMEM((2, 4, 16, 1024), BF),
            pltpu.VMEM((2, 2, 16, 512), BF),
            pltpu.VMEM((2, 2, 16, 1024), BF),
            pltpu.VMEM((3, 2, 32, 128), BF),
            pltpu.VMEM((2, 2, 32, 128), BF),
            pltpu.VMEM((8, D), F32),
            pltpu.VMEM((5, 8, 128), F32),
            pltpu.VMEM((10, 8, 128), F32),
            pltpu.SemaphoreType.DMA((6,)),
            pltpu.SemaphoreType.DMA((1,)),
            pltpu.SemaphoreType.DMA((N_SEM,)),
            pltpu.SemaphoreType.DMA((N_SEM,)),
            pltpu.SemaphoreType.DMA((2, NCH)),
            pltpu.SemaphoreType.DMA((2, NCH)),
        ],
        compiler_params=pltpu.CompilerParams(
            collective_id=0, has_side_effects=True, vmem_limit_bytes=60 * 1024 * 1024
        ),
    )(
        pair_live[0],
        block_input.reshape(TOK, D),
        cotangent.reshape(TOK, D),
        w_up,
        w_down,
        ln_gain.reshape(1, D),
        row_interp[0, 0],
        col_interp[0, 0],
    )
    lanes = 256
    source = pl.pallas_call(
        back,
        name="back",
        grid=(D // lanes,),
        out_shape=sds((48, 48, D), BF),
        in_specs=[pl.BlockSpec((3, 2, 32, 128), lambda i: (0, 0, 0, 0))]
        + [pl.BlockSpec((TOK, lanes), lambda i: (0, i))] * 3,
        out_specs=pl.BlockSpec((48, 48, lanes), lambda i: (0, 0, i)),
        scratch_shapes=[
            pltpu.VMEM((3, 384, 256), BF),
            pltpu.VMEM((384, 768), BF),
            pltpu.VMEM((6, 768, lanes), BF),
        ],
        compiler_params=pltpu.CompilerParams(dimension_semantics=("arbitrary",)),
    )(mats, ga, gg, gb)
    return source, up, down, gain.reshape(8)


def solution(mesh):
    in_specs = (
        P("row", "zone", None),
        P("row", "zone", None),
        P(),
        P(),
        P(),
        P("row", "zone", None),
        P("row", "zone", None, None, None),
        P("row", "zone", None, None, None),
    )
    out_specs = (
        P("row", "zone", None),
        P(("zone", "row"), None),
        P(("zone", "row"), None),
        P(("zone", "row")),
    )
    return jax.shard_map(
        on_device, mesh=mesh, in_specs=in_specs, out_specs=out_specs, check_vma=False
    )
```

```python
import functools
import math

import jax
import jax.numpy as jnp
from jax import lax
from jax.experimental import pallas as pl
from jax.experimental.pallas import tpu as pltpu
from jax.sharding import PartitionSpec as P

MESH = pl.DeviceIdType.MESH
BF = jnp.bfloat16
F32 = jnp.float32
ROOT_HALF = 0.7071067811865476
INV_ROOT_TAU = 0.3989422804014327
EPS = 1e-05
D = 1024
FF = 2048
TOK = 1024
CH = 256
NCH = TOK // CH
FB = 1024
NB = 1024
LN = 512
N_SEM = 64
N_RELAY = 2


def nt(a, b):
    return lax.dot_general(a, b, (((1,), (1,)), ((), ())), preferred_element_type=F32)


def tn(a, b):
    return lax.dot_general(a, b, (((0,), (0,)), ((), ())), preferred_element_type=F32)


def nn(a, b):
    return lax.dot_general(a, b, (((1,), (0,)), ((), ())), preferred_element_type=F32)


def front(
    factor,
    live_ref,
    x_hbm,
    ct_hbm,
    wu_hbm,
    wd_hbm,
    gain_ref,
    rowi_ref,
    coli_ref,
    gg_out,
    ga_out,
    gb_out,
    mats_out,
    up_out,
    down_out,
    gain_out,
    xv,
    ct,
    wu,
    wd,
    normed,
    normed_t,
    act_t,
    bp,
    gg,
    normal,
    inv_s,
    bn_s,
    grad,
    part,
    xa,
    xb,
    tt,
    ya,
    yb,
    uu,
    za,
    zb,
    mats,
    mrecv,
    gacc,
    gsrc,
    grecv,
    in_sem,
    out_sem,
    send_sem,
    recv_sem,
    halo_send,
    halo_recv,
    relay,
    relay_send,
    relay_recv,
):
    zone = lax.axis_index("zone")
    row = lax.axis_index("row")
    x = zone // 2
    c = zone - 2 * x
    y = row // 4
    z = row - 4 * y

    def mod4(v):
        return lax.rem(v, 4)

    def dx(j):
        return (2 * mod4(x + j) + c, row)

    def dy(j):
        return (zone, 4 * mod4(y + j) + z)

    def dz(j):
        return (zone, 4 * y + mod4(z + j))

    pair = (2 * x + (1 - c), row)
    upper = (zone, lax.rem(row + 1, 16))
    lower = (zone, lax.rem(row + 15, 16))

    loads = []
    for n, (src, dst) in enumerate(
        [(x_hbm.at[pl.ds(0, CH)], xv.at[pl.ds(0, CH)]), (wu_hbm, wu),
         (ct_hbm.at[pl.ds(0, CH)], ct.at[pl.ds(0, CH)]), (wd_hbm, wd),
         (x_hbm.at[pl.ds(CH, TOK - CH)], xv.at[pl.ds(CH, TOK - CH)]),
         (ct_hbm.at[pl.ds(CH, TOK - CH)], ct.at[pl.ds(CH, TOK - CH)])]
    ):
        cp = pltpu.make_async_copy(src, dst, in_sem.at[n])
        cp.start()
        loads.append(cp)

    barrier = pltpu.get_barrier_semaphore()
    peers = [pair, upper, lower] + [f(j) for f in (dx, dy, dz) for j in (1, 2, 3)]
    for peer in peers:
        pl.semaphore_signal(barrier, inc=1, device_id=peer, device_id_type=MESH)

    counter = [0]

    def remote(src, dst, device):
        k = counter[0]
        counter[0] += 1
        return pltpu.make_async_remote_copy(
            src_ref=src, dst_ref=dst, send_sem=send_sem.at[k], recv_sem=recv_sem.at[k],
            device_id=device, device_id_type=MESH,
        )

    mats[...] = jnp.zeros_like(mats)
    for k in range(3):
        keep = live_ref[0, k]
        if k == 0:
            keep = jnp.where(row > 0, keep, 0)
        if k == 2:
            keep = jnp.where(row < 15, keep, 0)
        mats[k, 0, :, 0:48] = (rowi_ref[k].astype(F32) * keep.astype(F32)).astype(BF)
        mats[k, 1, :, 0:48] = coli_ref[k]
    gacc[...] = jnp.zeros_like(gacc)

    def forward(start, m):
        gain = gain_ref[...]
        base = start % 512

        for s in range(m // CH):
            r0, r1 = base + s * CH, start + s * CH
            v = xv[r1 : r1 + CH, :].astype(F32)
            center = jnp.mean(v, -1, keepdims=True)
            sh = v - center
            inv = lax.rsqrt(jnp.mean(sh * sh, -1, keepdims=True) + EPS)
            nv = sh * inv
            normal[r0 : r0 + CH, :] = nv
            inv_s[r0 : r0 + CH, :] = jnp.broadcast_to(inv, (CH, 128))
            nb = (nv * gain).astype(BF)
            normed[r0 : r0 + CH, :] = nb
            normed_t[:, r1 : r1 + CH] = nb.T

        @pl.loop(0, FF // FB)
        def _(f):
            cols = pl.ds(pl.multiple_of(f * FB, FB), FB)
            pre = nn(normed[base : base + m, :], wu[:, cols])
            ba = nt(ct[start : start + m, :], wd[cols, :])
            h = 0.5 * (1.0 + lax.erf(pre * ROOT_HALF))
            act_t[pl.ds(4 * f, 4), :, :, start : start + m] = (pre * h).astype(BF).T.reshape(4, 4, 64, m)
            bp[start : start + m, cols] = (
                ba * (h + pre * jnp.exp(-0.5 * pre * pre) * INV_ROOT_TAU)
            ).astype(BF)

    def backward(start):
        gain = gain_ref[...]
        base = start % 512

        @pl.loop(0, D // NB)
        def _(f):
            cols = pl.ds(pl.multiple_of(f * NB, NB), NB)
            bn_s[:, cols] = nt(bp[start : start + CH, :], wu[cols, :])

        bn = bn_s[...]
        nv = normal[base : base + CH, :]
        inv = inv_s[base : base + CH, 0:1]
        gacc[...] += jnp.sum((bn * nv).reshape(CH // 8, 8, D), axis=0)
        scaled = bn * gain
        m1 = jnp.mean(scaled, -1, keepdims=True)
        m2 = jnp.mean(scaled * nv, -1, keepdims=True)
        g = ct[start : start + CH, :].astype(F32) + inv * (scaled - m1 - nv * m2)
        gg[start : start + CH, :] = g.astype(BF)

    def tokens(t):
        return pl.ds(t * CH, CH)

    def hop(src, dst, send, recv, device):
        return pltpu.make_async_remote_copy(
            src_ref=src, dst_ref=dst, send_sem=send, recv_sem=recv,
            device_id=device, device_id_type=MESH)

    def halo(t):
        src = gg.at[tokens(t)]
        return (
            hop(src, ga_out.at[tokens(t)], halo_send.at[0, t], halo_recv.at[0, t], lower),
            hop(src, gb_out.at[tokens(t)], halo_send.at[1, t], halo_recv.at[1, t], upper),
        )

    def halo_start(t):
        src = gg.at[tokens(t)]
        to_lower, to_upper = halo(t)
        if t >= N_RELAY:
            to_lower.start()
            to_upper.start()
            return

        @pl.when(z > 0)
        def _():
            to_lower.start()

        @pl.when(z == 0)
        def _():
            hop(src, relay.at[t], halo_send.at[0, t], relay_recv.at[t], dz(3)).start()

        @pl.when(z < 3)
        def _():
            to_upper.start()

        @pl.when(z == 3)
        def _():
            hop(src, relay.at[t], halo_send.at[1, t], relay_recv.at[t], dz(1)).start()

    def relays(t):
        down = hop(relay.at[t], ga_out.at[tokens(t)], relay_send.at[t], halo_recv.at[0, t], dy(3))
        up = hop(relay.at[t], gb_out.at[tokens(t)], relay_send.at[t], halo_recv.at[1, t], dy(1))
        land = hop(relay.at[t], relay.at[t], relay_send.at[t], relay_recv.at[t], dz(1))
        return down, up, land

    def relay_step(t):
        down, up, land = relays(t)

        @pl.when(z == 0)
        def _():
            land.wait_recv()
            up.start()

        @pl.when(z == 3)
        def _():
            land.wait_recv()
            down.start()

    for cp in loads[:4]:
        cp.wait()
    forward(0, CH)
    backward(0)
    pl.semaphore_wait(barrier, len(peers))
    m_low = remote(mats.at[0], mrecv.at[0], lower)
    m_upp = remote(mats.at[2], mrecv.at[1], upper)
    m_low.start()
    m_upp.start()
    halo_start(0)
    for cp in loads[4:]:
        cp.wait()
    forward(CH, CH)
    backward(CH)
    halo_start(1)
    forward(2 * CH, 2 * CH)

    at = ((x, y), (y, x))
    to = ((dx, dy), (dy, dx))
    order = [[mod4(at[s][0] + j) for j in (2, 1, 3, 0)] for s in range(2)]

    def up_tiles(ta, tb):
        fa = pl.ds(pl.multiple_of(ta * 256, 256), 256)
        fb = pl.ds(pl.multiple_of(tb * 256, 256), 256)

        @pl.loop(0, 1024 // LN)
        def _(n):
            la = pl.ds(pl.multiple_of(n * LN, LN), LN)
            lb = pl.ds(pl.multiple_of(1024 + n * LN, LN), LN)
            lhs = jnp.concatenate([normed_t[fa, :], normed_t[fb, :]], axis=0)
            left = nn(lhs, bp[:, la]).reshape(2, 2, 4, 4, 8, LN)
            right = nn(lhs, bp[:, lb]).reshape(2, 2, 4, 4, 8, LN)
            both = jnp.concatenate([left, right], axis=4).astype(BF)
            for cc in range(2):
                grad[0, cc, ta, :, :, :, la] = both[0, cc]
                grad[0, cc, tb, :, :, :, la] = both[1, cc]

    def down_tile(ty):
        @pl.loop(0, 1024 // LN)
        def _(n):
            la = pl.ds(pl.multiple_of(n * LN, LN), LN)
            v = nn(act_t[:, ty].reshape(512, TOK), ct[:, la])
            v = v.reshape(4, 2, 4, 16, LN).astype(BF)
            for cc in range(2):
                grad[1, cc, ty, :, :, :, la] = v[:, cc]

    def add_to(out, srcs, n):
        @pl.loop(0, n)
        def _(i):
            v = srcs[0][i].astype(F32)
            for s in srcs[1:]:
                v = v + s[i].astype(F32)
            out[i] = v.astype(BF)

    def add_into(dst, src, n):
        add_to(dst, [dst, src], n)

    zm, zp = mod4(z + 3), mod4(z + 1)
    p0 = [[None] * 4, [None] * 4]
    stage = [dict(), dict()]
    started = []

    def go(cp):
        cp.start()
        started.append(cp)
        return cp

    def send_pair(s, q):
        p0[s][q] = go(remote(grad.at[s, 1 - c, order[s][q]], part.at[s, q], pair))

    def merge(s, q):
        p0[s][q].wait_recv()
        add_into(grad.at[s, c, order[s][q]], part.at[s, q], 4)

    def a_first(s):
        far = grad.at[s, c, order[s][0]]
        peer = to[s][0]
        stage[s]["a1"] = [
            go(remote(far.at[pl.ds(0, 2)], xa.at[s, 0], peer(3))),
            go(remote(far.at[pl.ds(2, 2)], xa.at[s, 1], peer(1))),
        ]

    def a_second(s):
        low, high = grad.at[s, c, order[s][2]], grad.at[s, c, order[s][1]]
        peer = to[s][0]
        stage[s]["a1"][0].wait_recv()
        add_into(low.at[pl.ds(0, 2)], xa.at[s, 0], 2)
        first = go(remote(low, xb.at[s, 0], peer(3)))
        stage[s]["a1"][1].wait_recv()
        add_into(high.at[pl.ds(2, 2)], xa.at[s, 1], 2)
        stage[s]["a2"] = [first, go(remote(high, xb.at[s, 1], peer(1)))]

    def a_done(s):
        for cp in stage[s]["a2"]:
            cp.wait_recv()
        add_to(tt.at[s], [grad.at[s, c, order[s][3]], xb.at[s, 0], xb.at[s, 1]], 4)

    def b_first(s):
        far, peer = tt.at[s, mod4(at[s][1] + 2)], to[s][1]
        stage[s]["b1"] = [
            go(remote(far.at[pl.ds(0, 2)], ya.at[s, 0], peer(3))),
            go(remote(far.at[pl.ds(2, 2)], ya.at[s, 1], peer(1))),
        ]

    def b_second(s):
        low, high = tt.at[s, mod4(at[s][1] + 3)], tt.at[s, mod4(at[s][1] + 1)]
        peer = to[s][1]
        stage[s]["b1"][0].wait_recv()
        add_into(low.at[pl.ds(0, 2)], ya.at[s, 0], 2)
        first = go(remote(low, yb.at[s, 0], peer(3)))
        stage[s]["b1"][1].wait_recv()
        add_into(high.at[pl.ds(2, 2)], ya.at[s, 1], 2)
        stage[s]["b2"] = [first, go(remote(high, yb.at[s, 1], peer(1)))]

    def b_done(s):
        for cp in stage[s]["b2"]:
            cp.wait_recv()
        add_to(uu.at[s], [tt.at[s, at[s][1]], yb.at[s, 0], yb.at[s, 1]], 4)

    def z_first(s):
        far = uu.at[s, mod4(z + 2)]
        stage[s]["za"] = [
            go(remote(far.at[:, pl.ds(0, 512)], za.at[s, 0], dz(3))),
            go(remote(far.at[:, pl.ds(512, 512)], za.at[s, 1], dz(1))),
        ]

    def z_second(s):
        low, high = uu.at[s, zm], uu.at[s, zp]
        stage[s]["za"][0].wait_recv()
        low[:, 0:512] = (low[:, 0:512].astype(F32) + za[s, 0].astype(F32)).astype(BF)
        first = go(remote(low, zb.at[s, 0], dz(3)))
        stage[s]["za"][1].wait_recv()
        high[:, 512:1024] = (high[:, 512:1024].astype(F32) + za[s, 1].astype(F32)).astype(BF)
        stage[s]["zb"] = [first, go(remote(high, zb.at[s, 1], dz(1)))]

    def z_done(s):
        for cp in stage[s]["zb"]:
            cp.wait_recv()
        v = (uu[s, z].astype(F32) + zb[s, 0].astype(F32) + zb[s, 1].astype(F32)) * factor
        if s == 0:
            up_out[:, 0:1024] = v[0:8]
            up_out[:, 1024:2048] = v[8:16]
        else:
            down_out[...] = v

    gstage = {}

    def gain_send(axis_no, peer_of):
        gstage[axis_no] = [
            go(remote(gsrc.at[axis_no], grecv.at[3 * axis_no - 2 + j], peer_of(j + 1))) for j in range(3)
        ]

    def gain_sum(axis_no):
        v = gsrc[axis_no]
        for j, cp in enumerate(gstage[axis_no]):
            cp.wait_recv()
            v = v + grecv[3 * axis_no - 2 + j]
        gsrc[axis_no + 1] = v

    up_tiles(order[0][0], order[0][1])
    send_pair(0, 0)
    send_pair(0, 1)
    down_tile(order[1][0])
    send_pair(1, 0)
    merge(0, 0)
    a_first(0)
    down_tile(order[1][1])
    send_pair(1, 1)
    merge(1, 0)
    a_first(1)
    relay_step(0)
    up_tiles(order[0][2], order[0][3])
    send_pair(0, 2)
    send_pair(0, 3)
    merge(0, 1)
    merge(1, 1)
    backward(2 * CH)
    halo_start(2)
    merge(0, 2)
    a_second(0)
    down_tile(order[1][2])
    send_pair(1, 2)
    down_tile(order[1][3])
    send_pair(1, 3)
    merge(0, 3)
    merge(1, 2)
    a_second(1)
    relay_step(1)
    backward(3 * CH)
    halo_start(3)
    merge(1, 3)
    own = pltpu.make_async_copy(gg, gg_out, out_sem.at[0])
    own.start()
    gv = jnp.sum(gacc[...], axis=0, keepdims=True)
    gsrc[0] = jnp.concatenate([gv[:, 128 * i : 128 * (i + 1)] for i in range(8)], axis=0)
    g0 = remote(gsrc.at[0], grecv.at[0], pair)
    g0.start()
    g0.wait_recv()
    gsrc[1] = gsrc[0] + grecv[0]
    gain_send(1, dx)
    a_done(0)
    b_first(0)
    a_done(1)
    b_first(1)
    gain_sum(1)
    gain_send(2, dy)
    b_second(0)
    b_second(1)
    gain_sum(2)
    gain_send(3, dz)
    b_done(0)
    z_first(0)
    b_done(1)
    z_first(1)
    z_second(0)
    z_second(1)
    gain_sum(3)
    z_done(0)
    z_done(1)

    sub = lax.broadcasted_iota(jnp.int32, (8, 128), 0)
    lane = lax.broadcasted_iota(jnp.int32, (8, 128), 1)
    line = jnp.sum(jnp.where(sub == zone, gsrc[4], 0.0), axis=0, keepdims=True)
    gain_out[...] = factor * jnp.sum(
        jnp.where(lane == 8 * row + sub, jnp.broadcast_to(line, (8, 128)), 0.0), axis=1, keepdims=True)

    m_low.wait()
    m_upp.wait()
    mats_out[0] = mrecv[0]
    mats_out[1] = mats[1]
    mats_out[2] = mrecv[1]
    for t in range(NCH):
        for cp in halo(t):
            cp.wait()
    for t in range(N_RELAY):
        land = relays(t)[2]

        @pl.when((z == 0) | (z == 3))
        def _():
            land.wait_send()
    own.wait()
    g0.wait_send()
    for cp in started:
        cp.wait_send()


def back(mats_ref, ga, gg, gb, out, b1, b2, half):
    @pl.when(pl.program_id(0) == 0)
    def _():
        r = lax.broadcasted_iota(jnp.int32, (384, 128), 0)
        q = lax.broadcasted_iota(jnp.int32, (384, 128), 1)
        pick_l = jnp.where(q == (r // 64) * 8 + r % 8, 1.0, 0.0).astype(BF)
        pick_m = jnp.where(q == r // 8, 1.0, 0.0).astype(BF)
        a = lax.broadcasted_iota(jnp.int32, (32, 256), 0)
        b = lax.broadcasted_iota(jnp.int32, (32, 256), 1)
        rep_j = jnp.where(b % 32 == a, 1.0, 0.0).astype(BF)
        rep_i = jnp.where(b // 8 == a, 1.0, 0.0).astype(BF)
        rr = lax.broadcasted_iota(jnp.int32, (384, 256), 0)
        cc = lax.broadcasted_iota(jnp.int32, (384, 256), 1)
        same_i = (rr // 8) % 8 == cc // 32
        same_l = rr % 8 == cc % 8
        for k in range(3):
            col = nt(pick_l, mats_ref[k, 1]).astype(BF)
            b1[k] = jnp.where(same_i, nn(col, rep_j), 0.0).astype(BF)
            rw = nt(pick_m, mats_ref[k, 0]).astype(BF)
            b2[:, k * 256 : (k + 1) * 256] = jnp.where(same_l, nn(rw, rep_i), 0.0).astype(BF)

    for k, src in enumerate((ga, gg, gb)):
        for g in range(4):
            h = nn(b1[k], src[g * 256 : (g + 1) * 256, :]).astype(BF)
            for lb in range(6):
                half[lb, k * 256 + g * 64 : k * 256 + (g + 1) * 64, :] = h[lb * 64 : (lb + 1) * 64]
    for lp in range(3):
        a = nn(b2[...], half[2 * lp]).reshape(48, 8, -1)
        b = nn(b2[...], half[2 * lp + 1]).reshape(48, 8, -1)
        out[:, lp * 16 : (lp + 1) * 16, :] = jnp.concatenate([a, b], axis=1).astype(BF)


def on_device(block_input, cotangent, w_up, w_down, ln_gain, pair_live, row_interp, col_interp):
    factor = 1.0 / math.sqrt(TOK * lax.axis_size("zone") * lax.axis_size("row"))
    hbm = pl.BlockSpec(memory_space=pl.ANY)
    vmem = pl.BlockSpec(memory_space=pltpu.VMEM)
    smem = pl.BlockSpec(memory_space=pltpu.SMEM)
    sds = jax.ShapeDtypeStruct
    grid_shape = sds((TOK, D), BF)
    gg, ga, gb, mats, up, down, gain = pl.pallas_call(
        functools.partial(front, factor),
        name="front",
        out_shape=(grid_shape, grid_shape, grid_shape, sds((3, 2, 32, 128), BF),
                   sds((8, FF), F32), sds((16, D), F32), sds((8, 1), F32)),
        in_specs=[smem, hbm, hbm, hbm, hbm, vmem, vmem, vmem],
        out_specs=(hbm, hbm, hbm, vmem, vmem, vmem, vmem),
        scratch_shapes=[
            pltpu.VMEM((TOK, D), BF),
            pltpu.VMEM((TOK, D), BF),
            pltpu.VMEM((D, FF), BF),
            pltpu.VMEM((FF, D), BF),
            pltpu.VMEM((512, D), BF),
            pltpu.VMEM((D, TOK), BF),
            pltpu.VMEM((8, 4, 64, TOK), BF),
            pltpu.VMEM((TOK, FF), BF),
            pltpu.VMEM((TOK, D), BF),
            pltpu.VMEM((512, D), F32),
            pltpu.VMEM((512, 128), F32),
            pltpu.VMEM((CH, D), F32),
            pltpu.VMEM((2, 2, 4, 4, 4, 16, 1024), BF),
            pltpu.VMEM((2, 4, 4, 4, 16, 1024), BF),
            pltpu.VMEM((2, 2, 2, 4, 16, 1024), BF),
            pltpu.VMEM((2, 2, 4, 4, 16, 1024), BF),
            pltpu.VMEM((2, 4, 4, 16, 1024), BF),
            pltpu.VMEM((2, 2, 2, 16, 1024), BF),
            pltpu.VMEM((2, 2, 4, 16, 1024), BF),
            pltpu.VMEM((2, 4, 16, 1024), BF),
            pltpu.VMEM((2, 2, 16, 512), BF),
            pltpu.VMEM((2, 2, 16, 1024), BF),
            pltpu.VMEM((3, 2, 32, 128), BF),
            pltpu.VMEM((2, 2, 32, 128), BF),
            pltpu.VMEM((8, D), F32),
            pltpu.VMEM((5, 8, 128), F32),
            pltpu.VMEM((10, 8, 128), F32),
            pltpu.SemaphoreType.DMA((6,)),
            pltpu.SemaphoreType.DMA((1,)),
            pltpu.SemaphoreType.DMA((N_SEM,)),
            pltpu.SemaphoreType.DMA((N_SEM,)),
            pltpu.SemaphoreType.DMA((2, NCH)),
            pltpu.SemaphoreType.DMA((2, NCH)),
            pltpu.VMEM((N_RELAY, CH, D), BF),
            pltpu.SemaphoreType.DMA((N_RELAY,)),
            pltpu.SemaphoreType.DMA((N_RELAY,)),
        ],
        compiler_params=pltpu.CompilerParams(
            collective_id=0, has_side_effects=True, vmem_limit_bytes=60 * 1024 * 1024
        ),
    )(
        pair_live[0],
        block_input.reshape(TOK, D),
        cotangent.reshape(TOK, D),
        w_up,
        w_down,
        ln_gain.reshape(1, D),
        row_interp[0, 0],
        col_interp[0, 0],
    )
    lanes = 256
    source = pl.pallas_call(
        back,
        name="back",
        grid=(D // lanes,),
        out_shape=sds((48, 48, D), BF),
        in_specs=[pl.BlockSpec((3, 2, 32, 128), lambda i: (0, 0, 0, 0))]
        + [pl.BlockSpec((TOK, lanes), lambda i: (0, i))] * 3,
        out_specs=pl.BlockSpec((48, 48, lanes), lambda i: (0, 0, i)),
        scratch_shapes=[
            pltpu.VMEM((3, 384, 256), BF),
            pltpu.VMEM((384, 768), BF),
            pltpu.VMEM((6, 768, lanes), BF),
        ],
        compiler_params=pltpu.CompilerParams(dimension_semantics=("arbitrary",)),
    )(mats, ga, gg, gb)
    return source, up, down, gain.reshape(8)


def solution(mesh):
    in_specs = (
        P("row", "zone", None),
        P("row", "zone", None),
        P(),
        P(),
        P(),
        P("row", "zone", None),
        P("row", "zone", None, None, None),
        P("row", "zone", None, None, None),
    )
    out_specs = (
        P("row", "zone", None),
        P(("zone", "row"), None),
        P(("zone", "row"), None),
        P(("zone", "row")),
    )
    return jax.shard_map(
        on_device, mesh=mesh, in_specs=in_specs, out_specs=out_specs, check_vma=False
    )
```

```python
import functools
import math

import jax
import jax.numpy as jnp
from jax import lax
from jax.experimental import pallas as pl
from jax.experimental.pallas import tpu as pltpu
from jax.sharding import PartitionSpec as P

MESH = pl.DeviceIdType.MESH
BF = jnp.bfloat16
F32 = jnp.float32
ROOT_HALF = 0.7071067811865476
INV_ROOT_TAU = 0.3989422804014327
EPS = 1e-05
D = 1024
FF = 2048
TOK = 1024
CH = 256
NCH = TOK // CH
FB = 1024
NB = 1024
LN = 512
N_SEM = 64
RELAY = (2,)


def nt(a, b):
    return lax.dot_general(a, b, (((1,), (1,)), ((), ())), preferred_element_type=F32)


def tn(a, b):
    return lax.dot_general(a, b, (((0,), (0,)), ((), ())), preferred_element_type=F32)


def nn(a, b):
    return lax.dot_general(a, b, (((1,), (0,)), ((), ())), preferred_element_type=F32)


def front(
    factor,
    live_ref,
    x_hbm,
    ct_hbm,
    wu_hbm,
    wd_hbm,
    gain_ref,
    rowi_ref,
    coli_ref,
    gg_out,
    ga_out,
    gb_out,
    mats_out,
    up_out,
    down_out,
    gain_out,
    xv,
    ct,
    wu,
    wd,
    normed,
    normed_t,
    act_t,
    bp,
    gg,
    normal,
    inv_s,
    bn_s,
    grad,
    part,
    xa,
    xb,
    tt,
    ya,
    yb,
    uu,
    za,
    zb,
    mats,
    mrecv,
    gacc,
    gsrc,
    grecv,
    in_sem,
    out_sem,
    send_sem,
    recv_sem,
    halo_send,
    halo_recv,
    relay,
    relay_send,
    relay_recv,
):
    zone = lax.axis_index("zone")
    row = lax.axis_index("row")
    x = zone // 2
    c = zone - 2 * x
    y = row // 4
    z = row - 4 * y

    def mod4(v):
        return lax.rem(v, 4)

    def dx(j):
        return (2 * mod4(x + j) + c, row)

    def dy(j):
        return (zone, 4 * mod4(y + j) + z)

    def dz(j):
        return (zone, 4 * y + mod4(z + j))

    pair = (2 * x + (1 - c), row)
    upper = (zone, lax.rem(row + 1, 16))
    lower = (zone, lax.rem(row + 15, 16))

    loads = []
    for n, (src, dst) in enumerate(
        [(x_hbm.at[pl.ds(0, CH)], xv.at[pl.ds(0, CH)]), (wu_hbm, wu),
         (ct_hbm.at[pl.ds(0, CH)], ct.at[pl.ds(0, CH)]), (wd_hbm, wd),
         (x_hbm.at[pl.ds(CH, TOK - CH)], xv.at[pl.ds(CH, TOK - CH)]),
         (ct_hbm.at[pl.ds(CH, TOK - CH)], ct.at[pl.ds(CH, TOK - CH)])]
    ):
        cp = pltpu.make_async_copy(src, dst, in_sem.at[n])
        cp.start()
        loads.append(cp)

    barrier = pltpu.get_barrier_semaphore()
    peers = [pair, upper, lower] + [f(j) for f in (dx, dy, dz) for j in (1, 2, 3)]
    for peer in peers:
        pl.semaphore_signal(barrier, inc=1, device_id=peer, device_id_type=MESH)

    counter = [0]

    def remote(src, dst, device):
        k = counter[0]
        counter[0] += 1
        return pltpu.make_async_remote_copy(
            src_ref=src, dst_ref=dst, send_sem=send_sem.at[k], recv_sem=recv_sem.at[k],
            device_id=device, device_id_type=MESH,
        )

    mats[...] = jnp.zeros_like(mats)
    for k in range(3):
        keep = live_ref[0, k]
        if k == 0:
            keep = jnp.where(row > 0, keep, 0)
        if k == 2:
            keep = jnp.where(row < 15, keep, 0)
        mats[k, 0, :, 0:48] = (rowi_ref[k].astype(F32) * keep.astype(F32)).astype(BF)
        mats[k, 1, :, 0:48] = coli_ref[k]
    gacc[...] = jnp.zeros_like(gacc)

    def norm(start, m):
        gain = gain_ref[...]
        base = start % 512

        for s in range(m // CH):
            r0, r1 = base + s * CH, start + s * CH
            v = xv[r1 : r1 + CH, :].astype(F32)
            center = jnp.mean(v, -1, keepdims=True)
            sh = v - center
            inv = lax.rsqrt(jnp.mean(sh * sh, -1, keepdims=True) + EPS)
            nv = sh * inv
            normal[r0 : r0 + CH, :] = nv
            inv_s[r0 : r0 + CH, :] = jnp.broadcast_to(inv, (CH, 128))
            nb = (nv * gain).astype(BF)
            normed[r0 : r0 + CH, :] = nb
            normed_t[:, r1 : r1 + CH] = nb.T

    def forward(start, m):
        base = start % 512

        @pl.loop(0, FF // FB)
        def _(f):
            cols = pl.ds(pl.multiple_of(f * FB, FB), FB)
            pre = nn(normed[base : base + m, :], wu[:, cols])
            ba = nt(ct[start : start + m, :], wd[cols, :])
            h = 0.5 * (1.0 + lax.erf(pre * ROOT_HALF))
            act_t[pl.ds(4 * f, 4), :, :, start : start + m] = (pre * h).astype(BF).T.reshape(4, 4, 64, m)
            bp[start : start + m, cols] = (
                ba * (h + pre * jnp.exp(-0.5 * pre * pre) * INV_ROOT_TAU)
            ).astype(BF)

    def backward(start):
        gain = gain_ref[...]
        base = start % 512

        @pl.loop(0, D // NB)
        def _(f):
            cols = pl.ds(pl.multiple_of(f * NB, NB), NB)
            bn_s[:, cols] = nt(bp[start : start + CH, :], wu[cols, :])

        bn = bn_s[...]
        nv = normal[base : base + CH, :]
        inv = inv_s[base : base + CH, 0:1]
        gacc[...] += jnp.sum((bn * nv).reshape(CH // 8, 8, D), axis=0)
        scaled = bn * gain
        m1 = jnp.mean(scaled, -1, keepdims=True)
        m2 = jnp.mean(scaled * nv, -1, keepdims=True)
        g = ct[start : start + CH, :].astype(F32) + inv * (scaled - m1 - nv * m2)
        gg[start : start + CH, :] = g.astype(BF)

    def tokens(t):
        return pl.ds(t * CH, CH)

    def hop(src, dst, send, recv, device):
        return pltpu.make_async_remote_copy(
            src_ref=src, dst_ref=dst, send_sem=send, recv_sem=recv,
            device_id=device, device_id_type=MESH)

    def halo(t):
        src = gg.at[tokens(t)]
        return (
            hop(src, ga_out.at[tokens(t)], halo_send.at[0, t], halo_recv.at[0, t], lower),
            hop(src, gb_out.at[tokens(t)], halo_send.at[1, t], halo_recv.at[1, t], upper),
        )

    def halo_start(t):
        src = gg.at[tokens(t)]
        to_lower, to_upper = halo(t)
        if t not in RELAY:
            to_lower.start()
            to_upper.start()
            return

        @pl.when(z > 0)
        def _():
            to_lower.start()

        @pl.when(z == 0)
        def _():
            hop(src, relay.at[RELAY.index(t)], halo_send.at[0, t], relay_recv.at[RELAY.index(t)], dz(3)).start()

        @pl.when(z < 3)
        def _():
            to_upper.start()

        @pl.when(z == 3)
        def _():
            hop(src, relay.at[RELAY.index(t)], halo_send.at[1, t], relay_recv.at[RELAY.index(t)], dz(1)).start()

    def halo_inner(t):
        to_lower, to_upper = halo(t)

        @pl.when(z > 0)
        def _():
            to_lower.start()

        @pl.when(z < 3)
        def _():
            to_upper.start()

    def halo_wrap(t):
        to_lower, to_upper = halo(t)

        @pl.when(z == 0)
        def _():
            to_lower.start()

        @pl.when(z == 3)
        def _():
            to_upper.start()

    def relays(t):
        down = hop(relay.at[RELAY.index(t)], ga_out.at[tokens(t)], relay_send.at[RELAY.index(t)], halo_recv.at[0, t], dy(3))
        up = hop(relay.at[RELAY.index(t)], gb_out.at[tokens(t)], relay_send.at[RELAY.index(t)], halo_recv.at[1, t], dy(1))
        land = hop(relay.at[RELAY.index(t)], relay.at[RELAY.index(t)], relay_send.at[RELAY.index(t)], relay_recv.at[RELAY.index(t)], dz(1))
        return down, up, land

    def relay_step(t):
        down, up, land = relays(t)

        @pl.when(z == 0)
        def _():
            land.wait_recv()
            up.start()

        @pl.when(z == 3)
        def _():
            land.wait_recv()
            down.start()

    loads[0].wait()
    norm(0, CH)
    for cp in loads[1:4]:
        cp.wait()
    forward(0, CH)
    backward(0)
    pl.semaphore_wait(barrier, len(peers))
    m_low = remote(mats.at[0], mrecv.at[0], lower)
    m_upp = remote(mats.at[2], mrecv.at[1], upper)
    m_low.start()
    m_upp.start()
    halo_start(0)
    for cp in loads[4:]:
        cp.wait()
    norm(CH, CH)
    forward(CH, CH)
    backward(CH)
    halo_start(1)
    norm(2 * CH, 2 * CH)
    forward(2 * CH, 2 * CH)

    at = ((x, y), (y, x))
    to = ((dx, dy), (dy, dx))
    order = [[mod4(at[s][0] + j) for j in (2, 1, 3, 0)] for s in range(2)]

    def up_tiles(ta, tb):
        fa = pl.ds(pl.multiple_of(ta * 256, 256), 256)
        fb = pl.ds(pl.multiple_of(tb * 256, 256), 256)

        @pl.loop(0, 1024 // LN)
        def _(n):
            la = pl.ds(pl.multiple_of(n * LN, LN), LN)
            lb = pl.ds(pl.multiple_of(1024 + n * LN, LN), LN)
            lhs = jnp.concatenate([normed_t[fa, :], normed_t[fb, :]], axis=0)
            left = nn(lhs, bp[:, la]).reshape(2, 2, 4, 4, 8, LN)
            right = nn(lhs, bp[:, lb]).reshape(2, 2, 4, 4, 8, LN)
            both = jnp.concatenate([left, right], axis=4).astype(BF)
            for cc in range(2):
                grad[0, cc, ta, :, :, :, la] = both[0, cc]
                grad[0, cc, tb, :, :, :, la] = both[1, cc]

    def down_tile(ty):
        @pl.loop(0, 1024 // LN)
        def _(n):
            la = pl.ds(pl.multiple_of(n * LN, LN), LN)
            v = nn(act_t[:, ty].reshape(512, TOK), ct[:, la])
            v = v.reshape(4, 2, 4, 16, LN).astype(BF)
            for cc in range(2):
                grad[1, cc, ty, :, :, :, la] = v[:, cc]

    def add_to(out, srcs, n):
        @pl.loop(0, n)
        def _(i):
            v = srcs[0][i].astype(F32)
            for s in srcs[1:]:
                v = v + s[i].astype(F32)
            out[i] = v.astype(BF)

    def add_into(dst, src, n):
        add_to(dst, [dst, src], n)

    zm, zp = mod4(z + 3), mod4(z + 1)
    p0 = [[None] * 4, [None] * 4]
    stage = [dict(), dict()]
    started = []

    def go(cp):
        cp.start()
        started.append(cp)
        return cp

    def send_pair(s, q):
        p0[s][q] = go(remote(grad.at[s, 1 - c, order[s][q]], part.at[s, q], pair))

    def merge(s, q):
        p0[s][q].wait_recv()
        add_into(grad.at[s, c, order[s][q]], part.at[s, q], 4)

    def a_first(s):
        far = grad.at[s, c, order[s][0]]
        peer = to[s][0]
        stage[s]["a1"] = [
            go(remote(far.at[pl.ds(0, 2)], xa.at[s, 0], peer(3))),
            go(remote(far.at[pl.ds(2, 2)], xa.at[s, 1], peer(1))),
        ]

    def a_second(s):
        low, high = grad.at[s, c, order[s][2]], grad.at[s, c, order[s][1]]
        peer = to[s][0]
        stage[s]["a1"][0].wait_recv()
        add_into(low.at[pl.ds(0, 2)], xa.at[s, 0], 2)
        first = go(remote(low, xb.at[s, 0], peer(3)))
        stage[s]["a1"][1].wait_recv()
        add_into(high.at[pl.ds(2, 2)], xa.at[s, 1], 2)
        stage[s]["a2"] = [first, go(remote(high, xb.at[s, 1], peer(1)))]

    def a_done(s):
        for cp in stage[s]["a2"]:
            cp.wait_recv()
        add_to(tt.at[s], [grad.at[s, c, order[s][3]], xb.at[s, 0], xb.at[s, 1]], 4)

    def b_first(s):
        far, peer = tt.at[s, mod4(at[s][1] + 2)], to[s][1]
        stage[s]["b1"] = [
            go(remote(far.at[pl.ds(0, 2)], ya.at[s, 0], peer(3))),
            go(remote(far.at[pl.ds(2, 2)], ya.at[s, 1], peer(1))),
        ]

    def b_second(s):
        low, high = tt.at[s, mod4(at[s][1] + 3)], tt.at[s, mod4(at[s][1] + 1)]
        peer = to[s][1]
        stage[s]["b1"][0].wait_recv()
        add_into(low.at[pl.ds(0, 2)], ya.at[s, 0], 2)
        first = go(remote(low, yb.at[s, 0], peer(3)))
        stage[s]["b1"][1].wait_recv()
        add_into(high.at[pl.ds(2, 2)], ya.at[s, 1], 2)
        stage[s]["b2"] = [first, go(remote(high, yb.at[s, 1], peer(1)))]

    def b_done(s):
        for cp in stage[s]["b2"]:
            cp.wait_recv()
        add_to(uu.at[s], [tt.at[s, at[s][1]], yb.at[s, 0], yb.at[s, 1]], 4)

    def z_first(s):
        far = uu.at[s, mod4(z + 2)]
        stage[s]["za"] = [
            go(remote(far.at[:, pl.ds(0, 512)], za.at[s, 0], dz(3))),
            go(remote(far.at[:, pl.ds(512, 512)], za.at[s, 1], dz(1))),
        ]

    def z_second(s):
        low, high = uu.at[s, zm], uu.at[s, zp]
        stage[s]["za"][0].wait_recv()
        low[:, 0:512] = (low[:, 0:512].astype(F32) + za[s, 0].astype(F32)).astype(BF)
        first = go(remote(low, zb.at[s, 0], dz(3)))
        stage[s]["za"][1].wait_recv()
        high[:, 512:1024] = (high[:, 512:1024].astype(F32) + za[s, 1].astype(F32)).astype(BF)
        stage[s]["zb"] = [first, go(remote(high, zb.at[s, 1], dz(1)))]

    def z_done(s):
        for cp in stage[s]["zb"]:
            cp.wait_recv()
        v = (uu[s, z].astype(F32) + zb[s, 0].astype(F32) + zb[s, 1].astype(F32)) * factor
        if s == 0:
            up_out[:, 0:1024] = v[0:8]
            up_out[:, 1024:2048] = v[8:16]
        else:
            down_out[...] = v

    gstage = {}

    def gain_send(axis_no, peer_of):
        gstage[axis_no] = [
            go(remote(gsrc.at[axis_no], grecv.at[3 * axis_no - 2 + j], peer_of(j + 1))) for j in range(3)
        ]

    def gain_sum(axis_no):
        v = gsrc[axis_no]
        for j, cp in enumerate(gstage[axis_no]):
            cp.wait_recv()
            v = v + grecv[3 * axis_no - 2 + j]
        gsrc[axis_no + 1] = v

    up_tiles(order[0][0], order[0][1])
    send_pair(0, 0)
    send_pair(0, 1)
    down_tile(order[1][0])
    send_pair(1, 0)
    merge(0, 0)
    a_first(0)
    down_tile(order[1][1])
    send_pair(1, 1)
    merge(1, 0)
    a_first(1)
    up_tiles(order[0][2], order[0][3])
    send_pair(0, 2)
    send_pair(0, 3)
    merge(0, 1)
    merge(1, 1)
    backward(2 * CH)
    halo_start(2)
    merge(0, 2)
    a_second(0)
    down_tile(order[1][2])
    send_pair(1, 2)
    down_tile(order[1][3])
    send_pair(1, 3)
    merge(0, 3)
    merge(1, 2)
    a_second(1)
    backward(3 * CH)
    halo_inner(3)
    own = pltpu.make_async_copy(gg, gg_out, out_sem.at[0])
    own.start()
    gv = jnp.sum(gacc[...], axis=0, keepdims=True)
    gsrc[0] = jnp.concatenate([gv[:, 128 * i : 128 * (i + 1)] for i in range(8)], axis=0)
    g0 = remote(gsrc.at[0], grecv.at[0], pair)
    g0.start()
    merge(1, 3)
    g0.wait_recv()
    gsrc[1] = gsrc[0] + grecv[0]
    gain_send(1, dx)
    a_done(0)
    b_first(0)
    a_done(1)
    b_first(1)
    gain_sum(1)
    gain_send(2, dy)
    b_second(0)
    b_second(1)
    relay_step(2)
    halo_wrap(3)
    gain_sum(2)
    gain_send(3, dz)
    b_done(0)
    z_first(0)
    b_done(1)
    z_first(1)
    z_second(0)
    z_second(1)
    gain_sum(3)
    z_done(0)
    z_done(1)

    sub = lax.broadcasted_iota(jnp.int32, (8, 128), 0)
    lane = lax.broadcasted_iota(jnp.int32, (8, 128), 1)
    line = jnp.sum(jnp.where(sub == zone, gsrc[4], 0.0), axis=0, keepdims=True)
    gain_out[...] = factor * jnp.sum(
        jnp.where(lane == 8 * row + sub, jnp.broadcast_to(line, (8, 128)), 0.0), axis=1, keepdims=True)

    m_low.wait()
    m_upp.wait()
    mats_out[0] = mrecv[0]
    mats_out[1] = mats[1]
    mats_out[2] = mrecv[1]
    for t in range(NCH):
        for cp in halo(t):
            cp.wait()
    for t in RELAY:
        land = relays(t)[2]

        @pl.when((z == 0) | (z == 3))
        def _():
            land.wait_send()
    own.wait()
    g0.wait_send()
    for cp in started:
        cp.wait_send()


def back(mats_ref, ga, gg, gb, out, b1, b2, half):
    @pl.when(pl.program_id(0) == 0)
    def _():
        r = lax.broadcasted_iota(jnp.int32, (384, 128), 0)
        q = lax.broadcasted_iota(jnp.int32, (384, 128), 1)
        pick_l = jnp.where(q == (r // 64) * 8 + r % 8, 1.0, 0.0).astype(BF)
        pick_m = jnp.where(q == r // 8, 1.0, 0.0).astype(BF)
        a = lax.broadcasted_iota(jnp.int32, (32, 256), 0)
        b = lax.broadcasted_iota(jnp.int32, (32, 256), 1)
        rep_j = jnp.where(b % 32 == a, 1.0, 0.0).astype(BF)
        rep_i = jnp.where(b // 8 == a, 1.0, 0.0).astype(BF)
        rr = lax.broadcasted_iota(jnp.int32, (384, 256), 0)
        cc = lax.broadcasted_iota(jnp.int32, (384, 256), 1)
        same_i = (rr // 8) % 8 == cc // 32
        same_l = rr % 8 == cc % 8
        for k in range(3):
            col = nt(pick_l, mats_ref[k, 1]).astype(BF)
            b1[k] = jnp.where(same_i, nn(col, rep_j), 0.0).astype(BF)
            rw = nt(pick_m, mats_ref[k, 0]).astype(BF)
            b2[:, k * 256 : (k + 1) * 256] = jnp.where(same_l, nn(rw, rep_i), 0.0).astype(BF)

    for k, src in enumerate((ga, gg, gb)):
        for g in range(4):
            h = nn(b1[k], src[g * 256 : (g + 1) * 256, :]).astype(BF)
            for lb in range(6):
                half[lb, k * 256 + g * 64 : k * 256 + (g + 1) * 64, :] = h[lb * 64 : (lb + 1) * 64]
    for lp in range(3):
        a = nn(b2[...], half[2 * lp]).reshape(48, 8, -1)
        b = nn(b2[...], half[2 * lp + 1]).reshape(48, 8, -1)
        out[:, lp * 16 : (lp + 1) * 16, :] = jnp.concatenate([a, b], axis=1).astype(BF)


def on_device(block_input, cotangent, w_up, w_down, ln_gain, pair_live, row_interp, col_interp):
    factor = 1.0 / math.sqrt(TOK * lax.axis_size("zone") * lax.axis_size("row"))
    hbm = pl.BlockSpec(memory_space=pl.ANY)
    vmem = pl.BlockSpec(memory_space=pltpu.VMEM)
    smem = pl.BlockSpec(memory_space=pltpu.SMEM)
    sds = jax.ShapeDtypeStruct
    grid_shape = sds((TOK, D), BF)
    gg, ga, gb, mats, up, down, gain = pl.pallas_call(
        functools.partial(front, factor),
        name="front",
        out_shape=(grid_shape, grid_shape, grid_shape, sds((3, 2, 32, 128), BF),
                   sds((8, FF), F32), sds((16, D), F32), sds((8, 1), F32)),
        in_specs=[smem, hbm, hbm, hbm, hbm, vmem, vmem, vmem],
        out_specs=(hbm, hbm, hbm, vmem, vmem, vmem, vmem),
        scratch_shapes=[
            pltpu.VMEM((TOK, D), BF),
            pltpu.VMEM((TOK, D), BF),
            pltpu.VMEM((D, FF), BF),
            pltpu.VMEM((FF, D), BF),
            pltpu.VMEM((512, D), BF),
            pltpu.VMEM((D, TOK), BF),
            pltpu.VMEM((8, 4, 64, TOK), BF),
            pltpu.VMEM((TOK, FF), BF),
            pltpu.VMEM((TOK, D), BF),
            pltpu.VMEM((512, D), F32),
            pltpu.VMEM((512, 128), F32),
            pltpu.VMEM((CH, D), F32),
            pltpu.VMEM((2, 2, 4, 4, 4, 16, 1024), BF),
            pltpu.VMEM((2, 4, 4, 4, 16, 1024), BF),
            pltpu.VMEM((2, 2, 2, 4, 16, 1024), BF),
            pltpu.VMEM((2, 2, 4, 4, 16, 1024), BF),
            pltpu.VMEM((2, 4, 4, 16, 1024), BF),
            pltpu.VMEM((2, 2, 2, 16, 1024), BF),
            pltpu.VMEM((2, 2, 4, 16, 1024), BF),
            pltpu.VMEM((2, 4, 16, 1024), BF),
            pltpu.VMEM((2, 2, 16, 512), BF),
            pltpu.VMEM((2, 2, 16, 1024), BF),
            pltpu.VMEM((3, 2, 32, 128), BF),
            pltpu.VMEM((2, 2, 32, 128), BF),
            pltpu.VMEM((8, D), F32),
            pltpu.VMEM((5, 8, 128), F32),
            pltpu.VMEM((10, 8, 128), F32),
            pltpu.SemaphoreType.DMA((6,)),
            pltpu.SemaphoreType.DMA((1,)),
            pltpu.SemaphoreType.DMA((N_SEM,)),
            pltpu.SemaphoreType.DMA((N_SEM,)),
            pltpu.SemaphoreType.DMA((2, NCH)),
            pltpu.SemaphoreType.DMA((2, NCH)),
            pltpu.VMEM((len(RELAY), CH, D), BF),
            pltpu.SemaphoreType.DMA((len(RELAY),)),
            pltpu.SemaphoreType.DMA((len(RELAY),)),
        ],
        compiler_params=pltpu.CompilerParams(
            collective_id=0, has_side_effects=True, vmem_limit_bytes=60 * 1024 * 1024
        ),
    )(
        pair_live[0],
        block_input.reshape(TOK, D),
        cotangent.reshape(TOK, D),
        w_up,
        w_down,
        ln_gain.reshape(1, D),
        row_interp[0, 0],
        col_interp[0, 0],
    )
    lanes = 256
    source = pl.pallas_call(
        back,
        name="back",
        grid=(D // lanes,),
        out_shape=sds((48, 48, D), BF),
        in_specs=[pl.BlockSpec((3, 2, 32, 128), lambda i: (0, 0, 0, 0))]
        + [pl.BlockSpec((TOK, lanes), lambda i: (0, i))] * 3,
        out_specs=pl.BlockSpec((48, 48, lanes), lambda i: (0, 0, i)),
        scratch_shapes=[
            pltpu.VMEM((3, 384, 256), BF),
            pltpu.VMEM((384, 768), BF),
            pltpu.VMEM((6, 768, lanes), BF),
        ],
        compiler_params=pltpu.CompilerParams(dimension_semantics=("arbitrary",)),
    )(mats, ga, gg, gb)
    return source, up, down, gain.reshape(8)


def solution(mesh):
    in_specs = (
        P("row", "zone", None),
        P("row", "zone", None),
        P(),
        P(),
        P(),
        P("row", "zone", None),
        P("row", "zone", None, None, None),
        P("row", "zone", None, None, None),
    )
    out_specs = (
        P("row", "zone", None),
        P(("zone", "row"), None),
        P(("zone", "row"), None),
        P(("zone", "row")),
    )
    return jax.shard_map(
        on_device, mesh=mesh, in_specs=in_specs, out_specs=out_specs, check_vma=False
    )
```

```python
import functools
import math

import jax
import jax.numpy as jnp
from jax import lax
from jax.experimental import pallas as pl
from jax.experimental.pallas import tpu as pltpu
from jax.sharding import PartitionSpec as P

MESH = pl.DeviceIdType.MESH
BF = jnp.bfloat16
F32 = jnp.float32
ROOT_HALF = 0.7071067811865476
INV_ROOT_TAU = 0.3989422804014327
EPS = 1e-05
D = 1024
FF = 2048
TOK = 1024
CH = 256
NCH = TOK // CH
FB = 1024
NB = 1024
LN = 512
N_SEM = 64
RELAY = (2,)


def nt(a, b):
    return lax.dot_general(a, b, (((1,), (1,)), ((), ())), preferred_element_type=F32)


def tn(a, b):
    return lax.dot_general(a, b, (((0,), (0,)), ((), ())), preferred_element_type=F32)


def nn(a, b):
    return lax.dot_general(a, b, (((1,), (0,)), ((), ())), preferred_element_type=F32)


def interp_blocks(b1, b2, mats):
    r = lax.broadcasted_iota(jnp.int32, (384, 128), 0)
    q = lax.broadcasted_iota(jnp.int32, (384, 128), 1)
    pick_l = jnp.where(q == (r // 64) * 8 + r % 8, 1.0, 0.0).astype(BF)
    pick_m = jnp.where(q == r // 8, 1.0, 0.0).astype(BF)
    a = lax.broadcasted_iota(jnp.int32, (32, 256), 0)
    b = lax.broadcasted_iota(jnp.int32, (32, 256), 1)
    rep_j = jnp.where(b % 32 == a, 1.0, 0.0).astype(BF)
    rep_i = jnp.where(b // 8 == a, 1.0, 0.0).astype(BF)
    rr = lax.broadcasted_iota(jnp.int32, (384, 256), 0)
    cc = lax.broadcasted_iota(jnp.int32, (384, 256), 1)
    same_i = (rr // 8) % 8 == cc // 32
    same_l = rr % 8 == cc % 8
    for k in range(3):
        col = nt(pick_l, mats[k][1]).astype(BF)
        b1[k] = jnp.where(same_i, nn(col, rep_j), 0.0).astype(BF)
        rw = nt(pick_m, mats[k][0]).astype(BF)
        b2[:, k * 256 : (k + 1) * 256] = jnp.where(same_l, nn(rw, rep_i), 0.0).astype(BF)


def front(
    factor,
    live_ref,
    x_hbm,
    ct_hbm,
    wu_hbm,
    wd_hbm,
    gain_ref,
    rowi_ref,
    coli_ref,
    half_out,
    b2_out,
    up_out,
    down_out,
    gain_out,
    xv,
    ct,
    wu,
    wd,
    normed,
    normed_t,
    act_t,
    bp,
    gg,
    normal,
    inv_s,
    bn_s,
    grad,
    part,
    xa,
    xb,
    tt,
    ya,
    yb,
    uu,
    za,
    zb,
    mats,
    mrecv,
    gacc,
    gsrc,
    grecv,
    in_sem,
    out_sem,
    send_sem,
    recv_sem,
    halo_send,
    halo_recv,
    relay,
    relay_send,
    relay_recv,
    ga,
    gb,
    b1,
    hs,
    hs_sem,
):
    zone = lax.axis_index("zone")
    row = lax.axis_index("row")
    x = zone // 2
    c = zone - 2 * x
    y = row // 4
    z = row - 4 * y

    def mod4(v):
        return lax.rem(v, 4)

    def dx(j):
        return (2 * mod4(x + j) + c, row)

    def dy(j):
        return (zone, 4 * mod4(y + j) + z)

    def dz(j):
        return (zone, 4 * y + mod4(z + j))

    pair = (2 * x + (1 - c), row)
    upper = (zone, lax.rem(row + 1, 16))
    lower = (zone, lax.rem(row + 15, 16))

    loads = []
    for n, (src, dst) in enumerate(
        [(x_hbm.at[pl.ds(0, CH)], xv.at[pl.ds(0, CH)]), (wu_hbm, wu),
         (ct_hbm.at[pl.ds(0, CH)], ct.at[pl.ds(0, CH)]), (wd_hbm, wd),
         (x_hbm.at[pl.ds(CH, TOK - CH)], xv.at[pl.ds(CH, TOK - CH)]),
         (ct_hbm.at[pl.ds(CH, TOK - CH)], ct.at[pl.ds(CH, TOK - CH)])]
    ):
        cp = pltpu.make_async_copy(src, dst, in_sem.at[n])
        cp.start()
        loads.append(cp)

    barrier = pltpu.get_barrier_semaphore()
    peers = [pair, upper, lower] + [f(j) for f in (dx, dy, dz) for j in (1, 2, 3)]
    for peer in peers:
        pl.semaphore_signal(barrier, inc=1, device_id=peer, device_id_type=MESH)

    counter = [0]

    def remote(src, dst, device):
        k = counter[0]
        counter[0] += 1
        return pltpu.make_async_remote_copy(
            src_ref=src, dst_ref=dst, send_sem=send_sem.at[k], recv_sem=recv_sem.at[k],
            device_id=device, device_id_type=MESH,
        )

    mats[...] = jnp.zeros_like(mats)
    for k in range(3):
        keep = live_ref[0, k]
        if k == 0:
            keep = jnp.where(row > 0, keep, 0)
        if k == 2:
            keep = jnp.where(row < 15, keep, 0)
        mats[k, 0, :, 0:48] = (rowi_ref[k].astype(F32) * keep.astype(F32)).astype(BF)
        mats[k, 1, :, 0:48] = coli_ref[k]
    gacc[...] = jnp.zeros_like(gacc)

    def norm(start, m):
        gain = gain_ref[...]
        base = start % 512

        for s in range(m // CH):
            r0, r1 = base + s * CH, start + s * CH
            v = xv[r1 : r1 + CH, :].astype(F32)
            center = jnp.mean(v, -1, keepdims=True)
            sh = v - center
            inv = lax.rsqrt(jnp.mean(sh * sh, -1, keepdims=True) + EPS)
            nv = sh * inv
            normal[r0 : r0 + CH, :] = nv
            inv_s[r0 : r0 + CH, :] = jnp.broadcast_to(inv, (CH, 128))
            nb = (nv * gain).astype(BF)
            normed[r0 : r0 + CH, :] = nb
            normed_t[:, r1 : r1 + CH] = nb.T

    def forward(start, m):
        base = start % 512

        @pl.loop(0, FF // FB)
        def _(f):
            cols = pl.ds(pl.multiple_of(f * FB, FB), FB)
            pre = nn(normed[base : base + m, :], wu[:, cols])
            ba = nt(ct[start : start + m, :], wd[cols, :])
            h = 0.5 * (1.0 + lax.erf(pre * ROOT_HALF))
            act_t[pl.ds(4 * f, 4), :, :, start : start + m] = (pre * h).astype(BF).T.reshape(4, 4, 64, m)
            bp[start : start + m, cols] = (
                ba * (h + pre * jnp.exp(-0.5 * pre * pre) * INV_ROOT_TAU)
            ).astype(BF)

    def backward(start):
        gain = gain_ref[...]
        base = start % 512

        @pl.loop(0, D // NB)
        def _(f):
            cols = pl.ds(pl.multiple_of(f * NB, NB), NB)
            bn_s[:, cols] = nt(bp[start : start + CH, :], wu[cols, :])

        bn = bn_s[...]
        nv = normal[base : base + CH, :]
        inv = inv_s[base : base + CH, 0:1]
        gacc[...] += jnp.sum((bn * nv).reshape(CH // 8, 8, D), axis=0)
        scaled = bn * gain
        m1 = jnp.mean(scaled, -1, keepdims=True)
        m2 = jnp.mean(scaled * nv, -1, keepdims=True)
        g = ct[start : start + CH, :].astype(F32) + inv * (scaled - m1 - nv * m2)
        gg[start : start + CH, :] = g.astype(BF)

    def tokens(t):
        return pl.ds(t * CH, CH)

    def hop(src, dst, send, recv, device):
        return pltpu.make_async_remote_copy(
            src_ref=src, dst_ref=dst, send_sem=send, recv_sem=recv,
            device_id=device, device_id_type=MESH)

    def halo(t):
        src = gg.at[tokens(t)]
        return (
            hop(src, ga.at[tokens(t)], halo_send.at[0, t], halo_recv.at[0, t], lower),
            hop(src, gb.at[tokens(t)], halo_send.at[1, t], halo_recv.at[1, t], upper),
        )

    def halo_start(t):
        src = gg.at[tokens(t)]
        to_lower, to_upper = halo(t)
        if t not in RELAY:
            to_lower.start()
            to_upper.start()
            return

        @pl.when(z > 0)
        def _():
            to_lower.start()

        @pl.when(z == 0)
        def _():
            hop(src, relay.at[RELAY.index(t)], halo_send.at[0, t], relay_recv.at[RELAY.index(t)], dz(3)).start()

        @pl.when(z < 3)
        def _():
            to_upper.start()

        @pl.when(z == 3)
        def _():
            hop(src, relay.at[RELAY.index(t)], halo_send.at[1, t], relay_recv.at[RELAY.index(t)], dz(1)).start()

    def halo_inner(t):
        to_lower, to_upper = halo(t)

        @pl.when(z > 0)
        def _():
            to_lower.start()

        @pl.when(z < 3)
        def _():
            to_upper.start()

    def halo_wrap(t):
        to_lower, to_upper = halo(t)

        @pl.when(z == 0)
        def _():
            to_lower.start()

        @pl.when(z == 3)
        def _():
            to_upper.start()

    def relays(t):
        down = hop(relay.at[RELAY.index(t)], ga.at[tokens(t)], relay_send.at[RELAY.index(t)], halo_recv.at[0, t], dy(3))
        up = hop(relay.at[RELAY.index(t)], gb.at[tokens(t)], relay_send.at[RELAY.index(t)], halo_recv.at[1, t], dy(1))
        land = hop(relay.at[RELAY.index(t)], relay.at[RELAY.index(t)], relay_send.at[RELAY.index(t)], relay_recv.at[RELAY.index(t)], dz(1))
        return down, up, land

    def relay_step(t):
        down, up, land = relays(t)

        @pl.when(z == 0)
        def _():
            land.wait_recv()
            up.start()

        @pl.when(z == 3)
        def _():
            land.wait_recv()
            down.start()

    loads[0].wait()
    norm(0, CH)
    for cp in loads[1:4]:
        cp.wait()
    forward(0, CH)
    backward(0)
    pl.semaphore_wait(barrier, len(peers))
    m_low = remote(mats.at[0], mrecv.at[0], lower)
    m_upp = remote(mats.at[2], mrecv.at[1], upper)
    m_low.start()
    m_upp.start()
    halo_start(0)
    for cp in loads[4:]:
        cp.wait()
    norm(CH, CH)
    forward(CH, CH)
    backward(CH)
    halo_start(1)
    norm(2 * CH, 2 * CH)
    forward(2 * CH, 2 * CH)

    at = ((x, y), (y, x))
    to = ((dx, dy), (dy, dx))
    order = [[mod4(at[s][0] + j) for j in (2, 1, 3, 0)] for s in range(2)]

    def up_tiles(ta, tb):
        fa = pl.ds(pl.multiple_of(ta * 256, 256), 256)
        fb = pl.ds(pl.multiple_of(tb * 256, 256), 256)

        @pl.loop(0, 1024 // LN)
        def _(n):
            la = pl.ds(pl.multiple_of(n * LN, LN), LN)
            lb = pl.ds(pl.multiple_of(1024 + n * LN, LN), LN)
            lhs = jnp.concatenate([normed_t[fa, :], normed_t[fb, :]], axis=0)
            left = nn(lhs, bp[:, la]).reshape(2, 2, 4, 4, 8, LN)
            right = nn(lhs, bp[:, lb]).reshape(2, 2, 4, 4, 8, LN)
            both = jnp.concatenate([left, right], axis=4).astype(BF)
            for cc in range(2):
                grad[0, cc, ta, :, :, :, la] = both[0, cc]
                grad[0, cc, tb, :, :, :, la] = both[1, cc]

    def down_tile(ty):
        @pl.loop(0, 1024 // LN)
        def _(n):
            la = pl.ds(pl.multiple_of(n * LN, LN), LN)
            v = nn(act_t[:, ty].reshape(512, TOK), ct[:, la])
            v = v.reshape(4, 2, 4, 16, LN).astype(BF)
            for cc in range(2):
                grad[1, cc, ty, :, :, :, la] = v[:, cc]

    def add_to(out, srcs, n):
        @pl.loop(0, n)
        def _(i):
            v = srcs[0][i].astype(F32)
            for s in srcs[1:]:
                v = v + s[i].astype(F32)
            out[i] = v.astype(BF)

    def add_into(dst, src, n):
        add_to(dst, [dst, src], n)

    zm, zp = mod4(z + 3), mod4(z + 1)
    p0 = [[None] * 4, [None] * 4]
    stage = [dict(), dict()]
    started = []

    def go(cp):
        cp.start()
        started.append(cp)
        return cp

    def send_pair(s, q):
        p0[s][q] = go(remote(grad.at[s, 1 - c, order[s][q]], part.at[s, q], pair))

    def merge(s, q):
        p0[s][q].wait_recv()
        add_into(grad.at[s, c, order[s][q]], part.at[s, q], 4)

    def a_first(s):
        far = grad.at[s, c, order[s][0]]
        peer = to[s][0]
        stage[s]["a1"] = [
            go(remote(far.at[pl.ds(0, 2)], xa.at[s, 0], peer(3))),
            go(remote(far.at[pl.ds(2, 2)], xa.at[s, 1], peer(1))),
        ]

    def a_second(s):
        low, high = grad.at[s, c, order[s][2]], grad.at[s, c, order[s][1]]
        peer = to[s][0]
        stage[s]["a1"][0].wait_recv()
        add_into(low.at[pl.ds(0, 2)], xa.at[s, 0], 2)
        first = go(remote(low, xb.at[s, 0], peer(3)))
        stage[s]["a1"][1].wait_recv()
        add_into(high.at[pl.ds(2, 2)], xa.at[s, 1], 2)
        stage[s]["a2"] = [first, go(remote(high, xb.at[s, 1], peer(1)))]

    def a_done(s):
        for cp in stage[s]["a2"]:
            cp.wait_recv()
        add_to(tt.at[s], [grad.at[s, c, order[s][3]], xb.at[s, 0], xb.at[s, 1]], 4)

    def b_first(s):
        far, peer = tt.at[s, mod4(at[s][1] + 2)], to[s][1]
        stage[s]["b1"] = [
            go(remote(far.at[pl.ds(0, 2)], ya.at[s, 0], peer(3))),
            go(remote(far.at[pl.ds(2, 2)], ya.at[s, 1], peer(1))),
        ]

    def b_second(s):
        low, high = tt.at[s, mod4(at[s][1] + 3)], tt.at[s, mod4(at[s][1] + 1)]
        peer = to[s][1]
        stage[s]["b1"][0].wait_recv()
        add_into(low.at[pl.ds(0, 2)], ya.at[s, 0], 2)
        first = go(remote(low, yb.at[s, 0], peer(3)))
        stage[s]["b1"][1].wait_recv()
        add_into(high.at[pl.ds(2, 2)], ya.at[s, 1], 2)
        stage[s]["b2"] = [first, go(remote(high, yb.at[s, 1], peer(1)))]

    def b_done(s):
        for cp in stage[s]["b2"]:
            cp.wait_recv()
        add_to(uu.at[s], [tt.at[s, at[s][1]], yb.at[s, 0], yb.at[s, 1]], 4)

    def z_first(s):
        far = uu.at[s, mod4(z + 2)]
        stage[s]["za"] = [
            go(remote(far.at[:, pl.ds(0, 512)], za.at[s, 0], dz(3))),
            go(remote(far.at[:, pl.ds(512, 512)], za.at[s, 1], dz(1))),
        ]

    def z_second(s):
        low, high = uu.at[s, zm], uu.at[s, zp]
        stage[s]["za"][0].wait_recv()
        low[:, 0:512] = (low[:, 0:512].astype(F32) + za[s, 0].astype(F32)).astype(BF)
        first = go(remote(low, zb.at[s, 0], dz(3)))
        stage[s]["za"][1].wait_recv()
        high[:, 512:1024] = (high[:, 512:1024].astype(F32) + za[s, 1].astype(F32)).astype(BF)
        stage[s]["zb"] = [first, go(remote(high, zb.at[s, 1], dz(1)))]

    def z_done(s):
        for cp in stage[s]["zb"]:
            cp.wait_recv()
        v = (uu[s, z].astype(F32) + zb[s, 0].astype(F32) + zb[s, 1].astype(F32)) * factor
        if s == 0:
            up_out[:, 0:1024] = v[0:8]
            up_out[:, 1024:2048] = v[8:16]
        else:
            down_out[...] = v

    half_copies = []

    def columns(k, g):
        slot = len(half_copies) % 4
        if len(half_copies) >= 4:
            half_copies[-4].wait()
        src = (ga, gg, gb)[k]
        h = nn(b1[k], src[g * CH : (g + 1) * CH, :]).astype(BF)
        hs[slot] = h.reshape(6, 64, D)
        cp = pltpu.make_async_copy(
            hs.at[slot], half_out.at[:, pl.ds(k * 256 + g * 64, 64), :], hs_sem.at[slot])
        cp.start()
        half_copies.append(cp)

    def received(t):
        for k, cp in ((0, halo(t)[0]), (2, halo(t)[1])):
            cp.wait_recv()
            columns(k, t)

    gstage = {}

    def gain_send(axis_no, peer_of):
        gstage[axis_no] = [
            go(remote(gsrc.at[axis_no], grecv.at[3 * axis_no - 2 + j], peer_of(j + 1))) for j in range(3)
        ]

    def gain_sum(axis_no):
        v = gsrc[axis_no]
        for j, cp in enumerate(gstage[axis_no]):
            cp.wait_recv()
            v = v + grecv[3 * axis_no - 2 + j]
        gsrc[axis_no + 1] = v

    up_tiles(order[0][0], order[0][1])
    send_pair(0, 0)
    send_pair(0, 1)
    down_tile(order[1][0])
    send_pair(1, 0)
    merge(0, 0)
    a_first(0)
    down_tile(order[1][1])
    send_pair(1, 1)
    merge(1, 0)
    a_first(1)
    up_tiles(order[0][2], order[0][3])
    send_pair(0, 2)
    send_pair(0, 3)
    merge(0, 1)
    merge(1, 1)
    backward(2 * CH)
    halo_start(2)
    merge(0, 2)
    a_second(0)
    down_tile(order[1][2])
    send_pair(1, 2)
    down_tile(order[1][3])
    send_pair(1, 3)
    merge(0, 3)
    merge(1, 2)
    a_second(1)
    backward(3 * CH)
    halo_inner(3)
    m_low.wait()
    m_upp.wait()
    interp_blocks(b1, b2_out, (mrecv.at[0], mats.at[1], mrecv.at[1]))
    for g in range(NCH):
        columns(1, g)
    gv = jnp.sum(gacc[...], axis=0, keepdims=True)
    gsrc[0] = jnp.concatenate([gv[:, 128 * i : 128 * (i + 1)] for i in range(8)], axis=0)
    g0 = remote(gsrc.at[0], grecv.at[0], pair)
    g0.start()
    merge(1, 3)
    g0.wait_recv()
    gsrc[1] = gsrc[0] + grecv[0]
    gain_send(1, dx)
    a_done(0)
    b_first(0)
    a_done(1)
    b_first(1)
    received(0)
    gain_sum(1)
    gain_send(2, dy)
    b_second(0)
    b_second(1)
    relay_step(2)
    halo_wrap(3)
    received(1)
    gain_sum(2)
    gain_send(3, dz)
    b_done(0)
    z_first(0)
    b_done(1)
    z_first(1)
    z_second(0)
    z_second(1)
    received(2)
    received(3)
    gain_sum(3)
    z_done(0)
    z_done(1)

    sub = lax.broadcasted_iota(jnp.int32, (8, 128), 0)
    lane = lax.broadcasted_iota(jnp.int32, (8, 128), 1)
    line = jnp.sum(jnp.where(sub == zone, gsrc[4], 0.0), axis=0, keepdims=True)
    gain_out[...] = factor * jnp.sum(
        jnp.where(lane == 8 * row + sub, jnp.broadcast_to(line, (8, 128)), 0.0), axis=1, keepdims=True)

    for t in range(NCH):
        for cp in halo(t):
            cp.wait_send()
    for cp in half_copies[-4:]:
        cp.wait()
    for t in RELAY:
        land = relays(t)[2]

        @pl.when((z == 0) | (z == 3))
        def _():
            land.wait_send()
    g0.wait_send()
    for cp in started:
        cp.wait_send()


def back(b2, half, out):
    for lp in range(3):
        a = nn(b2[...], half[2 * lp]).reshape(48, 8, -1)
        b = nn(b2[...], half[2 * lp + 1]).reshape(48, 8, -1)
        out[:, lp * 16 : (lp + 1) * 16, :] = jnp.concatenate([a, b], axis=1).astype(BF)


def on_device(block_input, cotangent, w_up, w_down, ln_gain, pair_live, row_interp, col_interp):
    factor = 1.0 / math.sqrt(TOK * lax.axis_size("zone") * lax.axis_size("row"))
    hbm = pl.BlockSpec(memory_space=pl.ANY)
    vmem = pl.BlockSpec(memory_space=pltpu.VMEM)
    smem = pl.BlockSpec(memory_space=pltpu.SMEM)
    sds = jax.ShapeDtypeStruct
    half, b2, up, down, gain = pl.pallas_call(
        functools.partial(front, factor),
        name="front",
        out_shape=(sds((6, 768, D), BF), sds((384, 768), BF),
                   sds((8, FF), F32), sds((16, D), F32), sds((8, 1), F32)),
        in_specs=[smem, hbm, hbm, hbm, hbm, vmem, vmem, vmem],
        out_specs=(hbm, vmem, vmem, vmem, vmem),
        scratch_shapes=[
            pltpu.VMEM((TOK, D), BF),
            pltpu.VMEM((TOK, D), BF),
            pltpu.VMEM((D, FF), BF),
            pltpu.VMEM((FF, D), BF),
            pltpu.VMEM((512, D), BF),
            pltpu.VMEM((D, TOK), BF),
            pltpu.VMEM((8, 4, 64, TOK), BF),
            pltpu.VMEM((TOK, FF), BF),
            pltpu.VMEM((TOK, D), BF),
            pltpu.VMEM((512, D), F32),
            pltpu.VMEM((512, 128), F32),
            pltpu.VMEM((CH, D), F32),
            pltpu.VMEM((2, 2, 4, 4, 4, 16, 1024), BF),
            pltpu.VMEM((2, 4, 4, 4, 16, 1024), BF),
            pltpu.VMEM((2, 2, 2, 4, 16, 1024), BF),
            pltpu.VMEM((2, 2, 4, 4, 16, 1024), BF),
            pltpu.VMEM((2, 4, 4, 16, 1024), BF),
            pltpu.VMEM((2, 2, 2, 16, 1024), BF),
            pltpu.VMEM((2, 2, 4, 16, 1024), BF),
            pltpu.VMEM((2, 4, 16, 1024), BF),
            pltpu.VMEM((2, 2, 16, 512), BF),
            pltpu.VMEM((2, 2, 16, 1024), BF),
            pltpu.VMEM((3, 2, 32, 128), BF),
            pltpu.VMEM((2, 2, 32, 128), BF),
            pltpu.VMEM((8, D), F32),
            pltpu.VMEM((5, 8, 128), F32),
            pltpu.VMEM((10, 8, 128), F32),
            pltpu.SemaphoreType.DMA((6,)),
            pltpu.SemaphoreType.DMA((1,)),
            pltpu.SemaphoreType.DMA((N_SEM,)),
            pltpu.SemaphoreType.DMA((N_SEM,)),
            pltpu.SemaphoreType.DMA((2, NCH)),
            pltpu.SemaphoreType.DMA((2, NCH)),
            pltpu.VMEM((len(RELAY), CH, D), BF),
            pltpu.SemaphoreType.DMA((len(RELAY),)),
            pltpu.SemaphoreType.DMA((len(RELAY),)),
            pltpu.VMEM((TOK, D), BF),
            pltpu.VMEM((TOK, D), BF),
            pltpu.VMEM((3, 384, 256), BF),
            pltpu.VMEM((4, 6, 64, D), BF),
            pltpu.SemaphoreType.DMA((4,)),
        ],
        compiler_params=pltpu.CompilerParams(
            collective_id=0, has_side_effects=True, vmem_limit_bytes=63 * 1024 * 1024
        ),
    )(
        pair_live[0],
        block_input.reshape(TOK, D),
        cotangent.reshape(TOK, D),
        w_up,
        w_down,
        ln_gain.reshape(1, D),
        row_interp[0, 0],
        col_interp[0, 0],
    )
    lanes = 256
    source = pl.pallas_call(
        back,
        name="back",
        grid=(D // lanes,),
        out_shape=sds((48, 48, D), BF),
        in_specs=[
            pl.BlockSpec((384, 768), lambda i: (0, 0)),
            pl.BlockSpec((6, 768, lanes), lambda i: (0, 0, i)),
        ],
        out_specs=pl.BlockSpec((48, 48, lanes), lambda i: (0, 0, i)),
        compiler_params=pltpu.CompilerParams(dimension_semantics=("arbitrary",)),
    )(b2, half)
    return source, up, down, gain.reshape(8)


def solution(mesh):
    in_specs = (
        P("row", "zone", None),
        P("row", "zone", None),
        P(),
        P(),
        P(),
        P("row", "zone", None),
        P("row", "zone", None, None, None),
        P("row", "zone", None, None, None),
    )
    out_specs = (
        P("row", "zone", None),
        P(("zone", "row"), None),
        P(("zone", "row"), None),
        P(("zone", "row")),
    )
    return jax.shard_map(
        on_device, mesh=mesh, in_specs=in_specs, out_specs=out_specs, check_vma=False
    )
```
